32 devices in a mesh: groups: 2 (over y), seq: 4 (over z), rep: 2 (over x), fsdp: 2 (over core).
Axes of the slice: x: 2, y: 2, z: 4, core: 2. Of those that a mesh axis runs over, the one named last changes fastest.
Arguments:
- activations: bfloat16 [8, 512, 2048], P(('groups', 'rep', 'fsdp'), 'seq'), parts along dimension 0, may hold values from -6 to 6
- queries: bfloat16 [8, 512, 2048], P(('groups', 'rep', 'fsdp'), 'seq'), parts along dimension 0, may hold values from -102 to 102
- key_weight: bfloat16 [2048, 512], P(('seq', 'fsdp')), may hold values from -0.125 to 0.125
- value_weight: bfloat16 [2048, 512], P(('seq', 'fsdp')), may hold values from -0.125 to 0.125
- segment_ids: int32 [8, 512], P(('groups', 'rep', 'fsdp'), 'seq'), parts along dimension 0, may hold values from 0 to 3, never falling along the last dimension, each value on 1 to 384 neighbouring positions
- out_grad: bfloat16 [8, 512, 2048], P(('groups', 'rep', 'fsdp'), 'seq'), parts along dimension 0, may hold values from -6 to 6
Outputs:
- context: bfloat16 [8, 512, 2048], P(('groups', 'rep', 'fsdp'), 'seq'), parts along dimension 0
- query_grad: bfloat16 [8, 512, 2048], P(('groups', 'rep', 'fsdp'), 'seq'), parts along dimension 0
- input_grad: bfloat16 [8, 512, 2048], P(('groups', 'rep', 'fsdp'), 'seq'), parts along dimension 0
- key_weight_grad: bfloat16 [4096, 512], P(('groups', 'seq', 'fsdp')), parts along dimension 0
- value_weight_grad: bfloat16 [4096, 512], P(('groups', 'seq', 'fsdp')), parts along dimension 0
The draws below stay inside these ranges and needn't reach their ends.
There are 2 independent parts, one for each index of `groups`. The reference program is written for one: setup_inputs(seed, part) draws one part's arguments, and reference() takes and returns one part's arrays. A program takes and returns all parts, laid end to end along the dimension named above; an argument that names none is the same for every part. Nothing has to cross between parts.
Inputs may be any that keep to these rules, and one draw needn't show every extreme that they name: `segment_ids`: document numbers never fall along a sequence; a document covers at most 384 positions.
All inputs are finite; a program needn't handle non-finite values.
Results may differ from the reference program's by a relative error of at most 0.025.
The reference program's roundings to bfloat16 on the way count: a program that leaves them out, or rounds other values in their place, can miss the bound.
Values may be sent and summed in bfloat16 or wider, within the bound.
No kernel may reach another device: no remote copies, remote signals or barrier semaphores. Data moves between devices by JAX's collectives and lax.ppermute only.
A program may use at most 64 MiB of HBM per device.

```python
import math
import jax
import jax.numpy as jnp
import numpy as np
from jax import lax

D = 2048
HEADS = 16
KV_HEADS = 4
HEAD_DIM = 128
TOK_DEV = 128
SEQ_LEN = 512
BATCH = 4
N_SEQ = 4


def draw_queries(key, part):
    first = jax.random.fold_in(key, 0)
    shape = (BATCH, SEQ_LEN, HEADS * HEAD_DIM)
    return jnp.clip(jax.random.normal(first, shape, jnp.float32), -6.0, 6.0).astype(jnp.bfloat16)


def with_spikes(drawn, stream_key, source, target, blocks, factor):
    owner, partner = [(jnp.arange(drawn.shape[axis_at]) // (drawn.shape[axis_at] // blocks)).reshape([-1 if axis == axis_at else 1 for axis in range(drawn.ndim)]) for axis_at in (source, target)]
    chosen = jax.random.permutation(stream_key, blocks)[partner]
    strong = (owner == chosen) | (owner == (partner + blocks // 2) % blocks)
    return jnp.where(strong, factor * drawn, drawn)


def shard_levels(own_key, shape, pieces, least, high):
    def one(axis_at, blocks):
        draws = jax.random.uniform(jax.random.fold_in(jax.random.fold_in(own_key, 6), axis_at), (blocks,), jnp.float32, least / len(pieces), high / len(pieces))
        return jnp.repeat(jnp.exp(draws), shape[axis_at] // blocks).reshape((-1,) + (1,) * (len(shape) - axis_at - 1))

    gain = one(*pieces[0])
    for cut in pieces[1:]:
        gain = gain * one(*cut)
    return gain


def profile(number_of, total, reach, lean):
    portions = [(1 << 20) // math.isqrt(rank ** lean) + 1 for rank in range(2, number_of + 1)]
    surplus, holding = total - reach - (number_of - 1), [1] * (number_of - 1)
    while surplus > 0:
        movable = [i for i in range(number_of - 1) if holding[i] < reach]
        pool, remaining = sum([portions[i] for i in movable]), surplus
        for i in movable:
            extra = min(reach - holding[i], max(1, remaining * portions[i] // pool), surplus)
            holding[i] = holding[i] + extra
            surplus = surplus - extra
    return np.array([reach] + holding)


def uneven(own_key, count, total, most, skew):
    if count == 2:
        one = jax.random.randint(own_key, (), max(1, total - most), min(most, total - 1) + 1)
        return jnp.stack([one, total - one])
    sizes = jnp.asarray(profile(count, total, most, skew), jnp.int32)
    couples = (count - 1) // 2
    donor, taker = sizes[1:1 + 2 * couples:2], sizes[2:2 + 2 * couples:2]
    room = jnp.minimum(donor - 1, most - taker)
    moved = jax.random.randint(jax.random.fold_in(own_key, 1), (couples,), 0, 1 << 20) % (room + 1)
    sizes = sizes.at[1:1 + 2 * couples:2].set(donor - moved).at[2:2 + 2 * couples:2].set(taker + moved)
    return sizes[jax.random.permutation(jax.random.fold_in(own_key, 2), count)]


def normal_values(own_key, extent, spread, bound, cuts=(), kind=jnp.bfloat16):
    factor_of = shard_levels(own_key, extent, cuts, -0.22, 0.18) if cuts else 1.0
    array = jax.random.normal(own_key, extent, jnp.float32) * spread * factor_of
    return jnp.minimum(jnp.maximum(array, -bound), bound).astype(kind)


def noise_with(rng, dims, spread, limit, cuts, heavy, kind=jnp.bfloat16):
    values = spread * jax.random.normal(rng, dims, jnp.float32)
    if cuts:
        values = values * shard_levels(rng, dims, cuts, -0.22, 0.18)
    return jnp.clip(with_spikes(values, jax.random.fold_in(rng, 3), *heavy), -limit, limit).astype(kind)


def setup_inputs(seed: int = 0, part: int = 0) -> dict:
    streams_of = jax.random.split(jax.random.key(seed), 7)
    part_splits = jax.random.split(jax.random.fold_in(streams_of[6], part), 7)
    activations = noise_with(part_splits[0], (BATCH, SEQ_LEN, D), 1.0, 6.0, ((0, 4), (1, 4)), (1, 2, 4, 2.0))
    queries = draw_queries(jax.random.fold_in(jax.random.fold_in(streams_of[6], part), 71), part)
    key_weight = normal_values(streams_of[2], (D, KV_HEADS * HEAD_DIM), D ** -0.5, 0.125, ((0, 8),))
    value_weight = normal_values(streams_of[3], (D, KV_HEADS * HEAD_DIM), D ** -0.5, 0.125, ((0, 8),))
    segment_ids = jax.vmap(lambda own: jnp.searchsorted(jnp.cumsum(uneven(own, 4, SEQ_LEN, 3 * SEQ_LEN // 4, 0)), jnp.arange(SEQ_LEN), side="right"))(jax.random.split(part_splits[4], BATCH)).reshape((BATCH, SEQ_LEN)).astype(jnp.int32)
    out_grad = normal_values(part_splits[5], (BATCH, SEQ_LEN, HEADS * HEAD_DIM), 1.0, 6.0, ((0, 4), (1, 4)))
    return dict(activations=activations, queries=queries, key_weight=key_weight, value_weight=value_weight, segment_ids=segment_ids, out_grad=out_grad)


def reference(activations, queries, key_weight, value_weight, segment_ids, out_grad):
    inv_root = 1.0 / math.sqrt(HEAD_DIM)
    kv_group = HEADS // KV_HEADS
    kv_width = KV_HEADS * HEAD_DIM
    positions = jnp.arange(SEQ_LEN, dtype=jnp.int32)
    causal = positions[None, :] <= positions[:, None]
    stacked = jnp.concatenate([key_weight, value_weight], axis=1)

    def one_sequence(parts):
        inputs, query_rows, seg_row, grad_rows = parts
        key_rows = jnp.dot(inputs, key_weight, preferred_element_type=jnp.float32).astype(jnp.bfloat16)
        value_rows = jnp.dot(inputs, value_weight, preferred_element_type=jnp.float32).astype(jnp.bfloat16)
        allowed = causal & (seg_row[None, :] == seg_row[:, None])
        query_heads = query_rows.reshape(SEQ_LEN, HEADS, HEAD_DIM).transpose(1, 0, 2)
        key_heads = jnp.repeat(key_rows.reshape(SEQ_LEN, KV_HEADS, HEAD_DIM), kv_group, axis=1).transpose(1, 0, 2)
        value_heads = jnp.repeat(value_rows.reshape(SEQ_LEN, KV_HEADS, HEAD_DIM), kv_group, axis=1).transpose(1, 0, 2)
        grad_heads = grad_rows.reshape(SEQ_LEN, HEADS, HEAD_DIM).transpose(1, 0, 2)

        def one_head(head_parts):
            query_head, key_head, value_head, grad_head = head_parts
            scores = jnp.dot(query_head, key_head.T, preferred_element_type=jnp.float32) * inv_root
            scores = jnp.where(allowed, scores, -jnp.inf)
            peak = lax.optimization_barrier(jnp.max(scores, axis=1, keepdims=True))
            log_total = peak + jnp.log(lax.optimization_barrier(jnp.sum(jnp.exp(scores - peak), axis=1, keepdims=True)))
            probs = jnp.exp(scores - log_total)
            probs_low = probs.astype(jnp.bfloat16)
            out_head = jnp.dot(probs_low, value_head, preferred_element_type=jnp.float32).astype(jnp.bfloat16)
            row_dots = lax.optimization_barrier(jnp.sum(grad_head.astype(jnp.float32) * out_head.astype(jnp.float32), axis=1, keepdims=True))
            prob_grad = jnp.dot(grad_head, value_head.T, preferred_element_type=jnp.float32)
            score_grad = (probs * (prob_grad - row_dots)).astype(jnp.bfloat16)
            head_query_grad = (jnp.dot(score_grad, key_head, preferred_element_type=jnp.float32) * inv_root).astype(jnp.bfloat16)
            head_key_grad = (jnp.dot(score_grad.T, query_head, preferred_element_type=jnp.float32) * inv_root).astype(jnp.bfloat16)
            head_value_grad = jnp.dot(probs_low.T, grad_head, preferred_element_type=jnp.float32).astype(jnp.bfloat16)
            return (out_head, head_query_grad, head_key_grad, head_value_grad)
        outs = lax.map(one_head, (query_heads, key_heads, value_heads, grad_heads))
        context = outs[0].transpose(1, 0, 2).reshape(SEQ_LEN, HEADS * HEAD_DIM)
        query_grad = outs[1].transpose(1, 0, 2).reshape(SEQ_LEN, HEADS * HEAD_DIM)
        key_sum = outs[2].astype(jnp.float32).reshape(KV_HEADS, kv_group, SEQ_LEN, HEAD_DIM).sum(axis=1)
        value_sum = outs[3].astype(jnp.float32).reshape(KV_HEADS, kv_group, SEQ_LEN, HEAD_DIM).sum(axis=1)
        key_grad = key_sum.astype(jnp.bfloat16).transpose(1, 0, 2).reshape(SEQ_LEN, kv_width)
        value_grad = value_sum.astype(jnp.bfloat16).transpose(1, 0, 2).reshape(SEQ_LEN, kv_width)
        grad_kv = jnp.concatenate([key_grad, value_grad], axis=1)
        input_grad = lax.dot_general(grad_kv, stacked, (((1,), (1,)), ((), ())), preferred_element_type=jnp.float32).astype(jnp.bfloat16)
        inputs_dev = inputs.astype(jnp.float32).reshape(N_SEQ, TOK_DEV, D)
        grad_dev = grad_kv.astype(jnp.float32).reshape(N_SEQ, TOK_DEV, 2 * kv_width)
        partials = jnp.einsum('std,ste->sde', inputs_dev, grad_dev, precision=lax.Precision.HIGHEST)
        rounded = lax.optimization_barrier(partials.astype(jnp.bfloat16))
        weight_part = lax.optimization_barrier(jnp.sum(rounded.astype(jnp.float32), axis=0))
        return (context, query_grad, input_grad, weight_part)
    results = lax.map(one_sequence, (activations, queries, segment_ids, out_grad))
    weight_total = lax.optimization_barrier(jnp.sum(results[3], axis=0)).astype(jnp.bfloat16)
    return (results[0], results[1], results[2], weight_total[:, :kv_width], weight_total[:, kv_width:])
```

```python
import functools
import math

import jax
import jax.numpy as jnp
from jax import lax
from jax.experimental import pallas as pl
from jax.experimental.pallas import tpu as pltpu
from jax.sharding import PartitionSpec as P

HEADS = 16
KV_HEADS = 4
HEAD_DIM = 128
KV_WIDTH = KV_HEADS * HEAD_DIM
GROUP = HEADS // KV_HEADS
LOG2E = 1.4426950408889634
MASKED = -1e30
VMEM_LIMIT = 56 * 1024 * 1024


def params(**kw):
    return pltpu.CompilerParams(vmem_limit_bytes=VMEM_LIMIT, **kw)


def vspec():
    return pl.BlockSpec(memory_space=pltpu.VMEM)


def sspec():
    return pl.BlockSpec(memory_space=pltpu.SMEM)


def assemble(full_ref, own_ref, other_ref, place, count, rows):
    z, c = place[0], place[1]
    for k in range(count):
        src = lax.rem(z - k + count, count)
        for ref, core in ((own_ref, c), (other_ref, 1 - c)):
            start = pl.multiple_of((src * 2 + core) * rows, rows)
            full_ref[pl.ds(start, rows), :] = ref[k * rows : (k + 1) * rows, :]


def project_kernel(place, x_own, x_next, w_own, w_other, out_own, out_next, full, *, count, rows):
    assemble(full, w_own, w_other, place, count, rows)
    w = full[...]
    out_own[...] = jnp.dot(x_own[...], w, preferred_element_type=jnp.float32).astype(jnp.bfloat16)
    out_next[...] = jnp.dot(x_next[...], w, preferred_element_type=jnp.float32).astype(jnp.bfloat16)


def project(place, x_own, x_next, w_own, w_other, count, rows):
    width = w_own.shape[1]
    out = jax.ShapeDtypeStruct((x_own.shape[0], width), jnp.bfloat16)
    return pl.pallas_call(
        functools.partial(project_kernel, count=count, rows=rows),
        in_specs=[sspec()] + [vspec()] * 4,
        out_specs=[vspec()] * 2,
        out_shape=[out, out],
        scratch_shapes=[pltpu.VMEM((2 * count * rows, width), jnp.bfloat16)],
        compiler_params=params(),
        name="project",
    )(place, x_own, x_next, w_own, w_other)


def nt(a, b):
    return lax.dot_general(a, b, (((1,), (1,)), ((), ())), preferred_element_type=jnp.float32)


def tn(a, b):
    return lax.dot_general(a, b, (((0,), (0,)), ((), ())), preferred_element_type=jnp.float32)


def attend_kernel(place, q_ref, do_ref, seg_col, seg_rows, *refs, count, block):
    same, cross = refs[:count], refs[count : 2 * count]
    ctx_ref, dq_ref = refs[2 * count : 2 * count + 2]
    dk_refs = refs[2 * count + 2 : 3 * count + 2]
    dv_refs = refs[3 * count + 2 : 4 * count + 2]
    bias = refs[4 * count + 2]
    inv_root = 1.0 / math.sqrt(HEAD_DIM)
    length = count * block

    @pl.when(pl.program_id(0) == 0)
    def _():
        cols = lax.broadcasted_iota(jnp.int32, (block, length), 1)
        rows = lax.broadcasted_iota(jnp.int32, (block, length), 0)
        ok = (seg_rows[...] == seg_col[...]) & ((cols <= rows) | (cols >= block))
        bias[...] = jnp.where(ok, 0.0, MASKED)

    even = place[2] == 0
    first = jnp.concatenate([r[...] for r in same], axis=0)
    second = jnp.concatenate([r[...] for r in cross], axis=0)
    key = jnp.where(even, first, second)
    value = jnp.where(even, second, first)

    def stack(ref):
        return jnp.concatenate(
            [ref[:, h * HEAD_DIM : (h + 1) * HEAD_DIM] for h in range(GROUP)], axis=0
        )

    def unstack(ref, val):
        for h in range(GROUP):
            ref[:, h * HEAD_DIM : (h + 1) * HEAD_DIM] = val[h * block : (h + 1) * block, :]

    q, do = stack(q_ref), stack(do_ref)
    s = nt(q, key) * (inv_root * LOG2E)
    s = (s.reshape(GROUP, block, length) + bias[...][None]).reshape(GROUP * block, length)
    e = jnp.exp2(s - jnp.max(s, axis=1, keepdims=True))
    p = e * (1.0 / jnp.sum(e, axis=1, keepdims=True))
    p_low = p.astype(jnp.bfloat16)
    ctx = jnp.dot(p_low, value, preferred_element_type=jnp.float32).astype(jnp.bfloat16)
    unstack(ctx_ref, ctx)
    dots = jnp.sum(do.astype(jnp.float32) * ctx.astype(jnp.float32), axis=1, keepdims=True)
    ds = (p * (nt(do, value) - dots)).astype(jnp.bfloat16)
    dq = jnp.dot(ds, key, preferred_element_type=jnp.float32) * inv_root
    unstack(dq_ref, dq.astype(jnp.bfloat16))
    dv = tn(p_low, do)
    dk = tn(ds, q) * inv_root
    for k in range(count):
        dk_refs[k][...] = dk[k * block : (k + 1) * block, :].astype(dk_refs[k].dtype)
        dv_refs[k][...] = dv[k * block : (k + 1) * block, :].astype(dv_refs[k].dtype)


def attend(place, q, do, seg_col, seg_rows, same, cross):
    block, width = q.shape
    count = len(same)
    wide = pl.BlockSpec((block, GROUP * HEAD_DIM), lambda g: (0, g))
    head = pl.BlockSpec((block, HEAD_DIM), lambda g: (0, g))
    rows = jax.ShapeDtypeStruct((block, width), jnp.bfloat16)
    own = jax.ShapeDtypeStruct((block, KV_WIDTH), jnp.float32)
    sent = jax.ShapeDtypeStruct((block, KV_WIDTH), jnp.bfloat16)
    parts = [own] + [sent] * (count - 1)
    outs = pl.pallas_call(
        functools.partial(attend_kernel, count=count, block=block),
        grid=(KV_HEADS,),
        in_specs=[
            sspec(),
            wide,
            wide,
            pl.BlockSpec((block, 1), lambda g: (0, 0)),
            pl.BlockSpec((1, count * block), lambda g: (0, 0)),
        ]
        + [head] * (2 * count),
        out_specs=[wide, wide] + [head] * (2 * count),
        out_shape=[rows, rows] + parts + parts,
        scratch_shapes=[pltpu.VMEM((block, count * block), jnp.float32)],
        compiler_params=params(dimension_semantics=("arbitrary",)),
        name="attend",
    )(place, q, do, seg_col, seg_rows, *same, *cross)
    return outs[0], outs[1], outs[2 : 2 + count], outs[2 + count :]


def input_grad_kernel(place, gk, gv, a_own, a_other, b_own, b_other, out, fa, fb, *, count, rows):
    assemble(fa, a_own, a_other, place, count, rows)
    assemble(fb, b_own, b_other, place, count, rows)
    even = place[2] == 0
    ga = jnp.where(even, gk[...], gv[...])
    gb = jnp.where(even, gv[...], gk[...])
    out[...] = (nt(ga, fa[...]) + nt(gb, fb[...])).astype(jnp.bfloat16)


def input_grad_of(place, gk, gv, a_own, a_other, b_own, b_other, count, rows):
    full = pltpu.VMEM((2 * count * rows, KV_WIDTH), jnp.bfloat16)
    return pl.pallas_call(
        functools.partial(input_grad_kernel, count=count, rows=rows),
        in_specs=[sspec()] + [vspec()] * 6,
        out_specs=vspec(),
        out_shape=jax.ShapeDtypeStruct((gk.shape[0], 2 * count * rows), jnp.bfloat16),
        scratch_shapes=[full, full],
        compiler_params=params(),
        name="input_grad",
    )(place, gk, gv, a_own, a_other, b_own, b_other)


def weight_grad_kernel(x_own, x_other, g_own, g_other, out):
    out[...] = (tn(x_own[...], g_own[...]) + tn(x_other[...], g_other[...])).astype(jnp.bfloat16)


def weight_grad_of(x_own, x_other, g_own, g_other):
    return pl.pallas_call(
        weight_grad_kernel,
        in_specs=[vspec()] * 4,
        out_specs=vspec(),
        out_shape=jax.ShapeDtypeStruct((x_own.shape[1], g_own.shape[1]), jnp.bfloat16),
        compiler_params=params(),
        name="weight_grad",
    )(x_own, x_other, g_own, g_other)


def body(activations, queries, key_weight, value_weight, segment_ids, out_grad):
    inputs = activations[0]
    block, width = inputs.shape
    rows = key_weight.shape[0]
    n = lax.axis_size("seq")
    reps = lax.axis_size("rep")
    z, r, c = lax.axis_index("seq"), lax.axis_index("rep"), lax.axis_index("fsdp")
    odd = lax.rem(r, 2)
    place = jnp.stack([z, c, odd]).astype(jnp.int32)

    def around(x, k):
        return lax.ppermute(x, "seq", [(i, (i + k) % n) for i in range(n)])

    def up(x, k):
        return lax.ppermute(x, "seq", [(i, i + k) for i in range(n - k)])

    def down(x, k):
        return lax.ppermute(x, "seq", [(i, i - k) for i in range(k, n)])

    def cross_up(x, k):
        pairs = [
            (i * reps + j, (i + k) * reps + (j ^ 1)) for i in range(n - k) for j in range(reps)
        ]
        return lax.ppermute(x, ("seq", "rep"), pairs)

    def partner(x):
        return lax.ppermute(x, "rep", [(j, j ^ 1) for j in range(reps)])

    def core(x):
        return lax.ppermute(x, "fsdp", [(0, 1), (1, 0)])

    half = jnp.where(odd == 0, key_weight, value_weight)
    w_own = jnp.concatenate([half] + [around(half, k) for k in range(1, n)], axis=0)
    w_other = core(w_own)
    x_next = partner(inputs)
    seg = segment_ids[0] + 1
    seg_rows = jnp.concatenate([seg] + [up(seg, k) for k in range(1, n)], axis=0)[None, :]
    seg_col = seg[:, None]

    columns = inputs.reshape(block, n, 2, rows)
    x_mine = lax.dynamic_index_in_dim(columns, c, 2, keepdims=False)
    x_theirs = core(lax.dynamic_index_in_dim(columns, 1 - c, 2, keepdims=False))
    x_both = jnp.concatenate([x_mine, x_theirs], axis=0)

    proj_own, proj_next = project(place, inputs, x_next, w_own, w_other, n, rows)
    same = [proj_own] + [up(proj_own, k) for k in range(1, n)]
    cross = [cross_up(proj_next, k) for k in range(n)]

    def take(k):
        return lax.dynamic_index_in_dim(x_both, lax.rem(z + k + n, n), 1, keepdims=False)

    x_low, _ = lax.optimization_barrier((x_both, proj_own))
    x_pieces = {0: take(0)}

    def piece(source, k):
        return lax.dynamic_index_in_dim(source, lax.rem(z + k + n, n), 1, keepdims=False)

    low = {k: down(piece(x_low, -k), k) for k in range(1, n)}

    context, query_grad, dk, dv = attend(
        place, queries[0], out_grad[0], seg_col, seg_rows, same, cross
    )
    back = [
        down(jnp.concatenate([dk[k], dv[k]], axis=1), k) for k in range(1, n)
    ]
    x_high, _ = lax.optimization_barrier((x_both, dk[1]))
    high = {k: up(piece(x_high, k), k) for k in range(1, n)}

    w_late, _ = lax.optimization_barrier((w_own, same[1]))
    b_own = partner(w_late)
    b_other = core(b_own)

    total = jnp.concatenate([dk[0], dv[0]], axis=1)
    for b in back:
        total = total + b.astype(jnp.float32)
    grad_kv = total.astype(jnp.bfloat16)
    g_own = jnp.concatenate([grad_kv] + [around(grad_kv, k) for k in range(1, n)], axis=0)
    g_other = core(g_own)
    input_grad = input_grad_of(
        place, grad_kv[:, :KV_WIDTH], grad_kv[:, KV_WIDTH:], w_own, w_other, b_own, b_other, n, rows
    )

    own_x, other_x = [x_pieces[0][:block]], [x_pieces[0][block:]]
    for k in range(1, n):
        got = jnp.where(z >= k, high[k], low[n - k])
        own_x.append(got[:block])
        other_x.append(got[block:])
    partial = weight_grad_of(
        jnp.concatenate(own_x, axis=0), jnp.concatenate(other_x, axis=0), g_own, g_other
    )
    if reps == 2:
        grad = partial.astype(jnp.float32) + partner(partial).astype(jnp.float32)
    else:
        grad = lax.psum(partial.astype(jnp.float32), "rep")
    grad = grad.astype(jnp.bfloat16)
    return (
        context[None],
        query_grad[None],
        input_grad[None],
        grad[:, :KV_WIDTH],
        grad[:, KV_WIDTH:],
    )


def solution(mesh):
    return jax.shard_map(
        body,
        mesh=mesh,
        in_specs=(
            P(("groups", "rep", "fsdp"), "seq", None),
            P(("groups", "rep", "fsdp"), "seq", None),
            P(("seq", "fsdp"), None),
            P(("seq", "fsdp"), None),
            P(("groups", "rep", "fsdp"), "seq"),
            P(("groups", "rep", "fsdp"), "seq", None),
        ),
        out_specs=(
            P(("groups", "rep", "fsdp"), "seq", None),
            P(("groups", "rep", "fsdp"), "seq", None),
            P(("groups", "rep", "fsdp"), "seq", None),
            P(("groups", "seq", "fsdp"), None),
            P(("groups", "seq", "fsdp"), None),
        ),
        check_vma=False,
    )
```

```python
import functools
import math

import jax
import jax.numpy as jnp
from jax import lax
from jax.experimental import pallas as pl
from jax.experimental.pallas import tpu as pltpu
from jax.sharding import PartitionSpec as P

HEADS = 16
KV_HEADS = 4
HEAD_DIM = 128
KV_WIDTH = KV_HEADS * HEAD_DIM
GROUP = HEADS // KV_HEADS
PARTS = 2
LOG2E = 1.4426950408889634
MASKED = -1e30
EXTRA = 16
VMEM_LIMIT = 56 * 1024 * 1024


def params(**kw):
    return pltpu.CompilerParams(vmem_limit_bytes=VMEM_LIMIT, **kw)


def vspec():
    return pl.BlockSpec(memory_space=pltpu.VMEM)


def sspec():
    return pl.BlockSpec(memory_space=pltpu.SMEM)


def assemble(full_ref, own_ref, other_ref, place, count, rows):
    z, c = place[0], place[1]
    for k in range(count):
        src = lax.rem(z - k + count, count)
        for ref, core in ((own_ref, c), (other_ref, 1 - c)):
            start = pl.multiple_of((src * 2 + core) * rows, rows)
            full_ref[pl.ds(start, rows), :] = ref[k * rows : (k + 1) * rows, :]


def project_kernel(
    place, seg, x_own, x_next, w_own, w_other, out_own, out_next, full, *, count, rows
):
    assemble(full, w_own, w_other, place, count, rows)
    w = full[...]
    block = x_own.shape[0]
    out_own[:block, :] = jnp.dot(x_own[...], w, preferred_element_type=jnp.float32).astype(
        jnp.bfloat16
    )
    ids = (seg[...] + 1).astype(jnp.float32)
    wide = jnp.concatenate([jnp.broadcast_to(ids, (EXTRA, block))] * (KV_WIDTH // block), axis=1)
    out_own[block:, :] = wide.astype(jnp.bfloat16)
    out_next[...] = jnp.dot(x_next[...], w, preferred_element_type=jnp.float32).astype(jnp.bfloat16)


def project(place, seg, x_own, x_next, w_own, w_other, count, rows):
    width = w_own.shape[1]
    block = x_own.shape[0]
    return pl.pallas_call(
        functools.partial(project_kernel, count=count, rows=rows),
        in_specs=[sspec()] + [vspec()] * 5,
        out_specs=[vspec()] * 2,
        out_shape=[
            jax.ShapeDtypeStruct((block + EXTRA, width), jnp.bfloat16),
            jax.ShapeDtypeStruct((block, width), jnp.bfloat16),
        ],
        scratch_shapes=[pltpu.VMEM((2 * count * rows, width), jnp.bfloat16)],
        compiler_params=params(),
        name="project",
    )(place, seg, x_own, x_next, w_own, w_other)


def pack_kernel(place, own, mate, *refs, count):
    cols, outs = refs[: count - 1], refs[count - 1 :]
    block, width = mate.shape
    half = width // PARTS
    first = jnp.concatenate([own[:block, :half], mate[:, :half]], axis=1)
    tail = own[block:, :]
    outs[0][:block, :] = first
    outs[0][block:, :] = tail
    outs[1][...] = jnp.concatenate([own[:block, half:], mate[:, half:]], axis=1)
    for k in range(1, count):
        goes_up = place[0] + k < count
        outs[k + 1][:block, :] = jnp.where(goes_up, first, cols[k - 1][...])
        outs[k + 1][block:, :] = jnp.where(goes_up, tail, jnp.zeros_like(tail))


def pack(place, own, mate, cols):
    count = len(cols) + 1
    tall = jax.ShapeDtypeStruct(own.shape, own.dtype)
    outs = pl.pallas_call(
        functools.partial(pack_kernel, count=count),
        in_specs=[sspec()] + [vspec()] * (count + 1),
        out_specs=[vspec()] * (count + 1),
        out_shape=[tall, jax.ShapeDtypeStruct(mate.shape, mate.dtype)] + [tall] * (count - 1),
        compiler_params=params(),
        name="pack",
    )(place, own, mate, *cols)
    return outs[0], outs[1], outs[2:]


def nt(a, b):
    return lax.dot_general(a, b, (((1,), (1,)), ((), ())), preferred_element_type=jnp.float32)


def tn(a, b):
    return lax.dot_general(a, b, (((0,), (0,)), ((), ())), preferred_element_type=jnp.float32)


def attend_kernel(place, q_ref, do_ref, *refs, count, block, opening):
    first, second = refs[:count], refs[count : 2 * count]
    refs = refs[2 * count :]
    if opening:
        seg_refs, cols = refs[:count], refs[count : 2 * count - 1]
        ctx_ref, dq_ref, bias = refs[2 * count - 1 : 2 * count + 2]
        grads, own_grad = refs[2 * count + 2 : 3 * count + 1], refs[-1]
    else:
        bias = refs[0]
        ctx_ref, dq_ref = refs[3:5]
        grads, own_grad = refs[5:-1], refs[-1]
    inv_root = 1.0 / math.sqrt(HEAD_DIM)
    length = count * block

    if opening:

        @pl.when(pl.program_id(0) == 0)
        def _():
            ids = [r[:1, :].astype(jnp.float32) for r in seg_refs]
            mine = jnp.broadcast_to(ids[0], (block, block)).T
            rows = lax.broadcasted_iota(jnp.int32, (block, block), 0)
            cols_here = lax.broadcasted_iota(jnp.int32, (block, block), 1)
            for k in range(count):
                ok = mine == jnp.broadcast_to(ids[k], (block, block))
                if k == 0:
                    ok = ok & (cols_here <= rows)
                bias[:, k * block : (k + 1) * block] = jnp.where(ok, 0.0, MASKED)

    even = place[2] == 0
    a = jnp.concatenate([r[...] for r in first], axis=0)
    b = jnp.concatenate([r[...] for r in second], axis=0)
    key = jnp.where(even, a, b)
    value = jnp.where(even, b, a)

    def stack(ref):
        return jnp.concatenate(
            [ref[:, h * HEAD_DIM : (h + 1) * HEAD_DIM] for h in range(GROUP)], axis=0
        )

    def unstack(ref, val):
        for h in range(GROUP):
            ref[:, h * HEAD_DIM : (h + 1) * HEAD_DIM] = val[h * block : (h + 1) * block, :]

    q, do = stack(q_ref), stack(do_ref)
    s = nt(q, key) * (inv_root * LOG2E)
    s = (s.reshape(GROUP, block, length) + bias[...][None]).reshape(GROUP * block, length)
    e = jnp.exp2(s - jnp.max(s, axis=1, keepdims=True))
    p = e * (1.0 / jnp.sum(e, axis=1, keepdims=True))
    p_low = p.astype(jnp.bfloat16)
    ctx = jnp.dot(p_low, value, preferred_element_type=jnp.float32).astype(jnp.bfloat16)
    unstack(ctx_ref, ctx)
    dots = jnp.sum(do.astype(jnp.float32) * ctx.astype(jnp.float32), axis=1, keepdims=True)
    ds = (p * (nt(do, value) - dots)).astype(jnp.bfloat16)
    dq = jnp.dot(ds, key, preferred_element_type=jnp.float32) * inv_root
    unstack(dq_ref, dq.astype(jnp.bfloat16))
    dv = tn(p_low, do)
    dk = tn(ds, q) * inv_root
    at_key = pl.multiple_of(pl.program_id(0) * HEAD_DIM, HEAD_DIM)
    at_value = pl.multiple_of(at_key + KV_WIDTH // PARTS, HEAD_DIM)
    own_grad[:, pl.ds(at_key, HEAD_DIM)] = dk[:block]
    own_grad[:, pl.ds(at_value, HEAD_DIM)] = dv[:block]
    for k in range(1, count):
        piece = slice(k * block, (k + 1) * block)
        for at, grad in ((at_key, dk), (at_value, dv)):
            sent = grad[piece].astype(jnp.bfloat16)
            if opening:
                sent = jnp.where(place[0] >= k, sent, cols[k - 1][:, pl.ds(at, HEAD_DIM)])
            grads[k - 1][:, pl.ds(at, HEAD_DIM)] = sent


def attend(place, q, do, pairs, part, cols, before):
    block, width = q.shape
    count = len(pairs)
    steps = KV_HEADS // PARTS
    opening = not before
    wide = pl.BlockSpec((block, GROUP * HEAD_DIM), lambda g: (0, part * steps + g))
    first = pl.BlockSpec((block, HEAD_DIM), lambda g: (0, g))
    second = pl.BlockSpec((block, HEAD_DIM), lambda g: (0, steps + g))
    both = 2 * KV_WIDTH // PARTS
    held = pl.BlockSpec((block, both), lambda g: (0, 0))
    bias = pl.BlockSpec((block, count * block), lambda g: (0, 0))
    seg = pl.BlockSpec((EXTRA, block), lambda g: (block // EXTRA, 0))
    rows = jax.ShapeDtypeStruct((block, width), jnp.bfloat16)
    own = jax.ShapeDtypeStruct((block, both), jnp.float32)
    sent = jax.ShapeDtypeStruct((block, both), jnp.bfloat16)
    operands = [place, q, do, *pairs, *pairs]
    in_specs = [sspec(), wide, wide] + [first] * count + [second] * count
    if opening:
        operands += [*pairs, *cols]
        in_specs += [seg] * count + [held] * (count - 1)
        out_specs = [wide, wide, bias] + [held] * count
        out_shape = [rows, rows, jax.ShapeDtypeStruct((block, count * block), jnp.float32)]
        aliases = {}
    else:
        context, query_grad, mask = before
        aliases = {len(operands) + 1: 0, len(operands) + 2: 1}
        operands += [mask, context, query_grad]
        in_specs += [bias] + [pl.BlockSpec(memory_space=pl.ANY)] * 2
        out_specs = [wide, wide] + [held] * count
        out_shape = [rows, rows]
    outs = pl.pallas_call(
        functools.partial(attend_kernel, count=count, block=block, opening=opening),
        grid=(steps,),
        in_specs=in_specs,
        out_specs=out_specs,
        out_shape=out_shape + [sent] * (count - 1) + [own],
        input_output_aliases=aliases,
        compiler_params=params(dimension_semantics=("arbitrary",)),
        name="attend",
    )(*operands)
    return outs[: len(outs) - count], outs[len(outs) - count : -1], outs[-1]


def input_grad_kernel(place, *refs, count, rows):
    grads = refs[:PARTS]
    a_own, a_other, b_own, b_other, out, fa, fb = refs[PARTS:]
    assemble(fa, a_own, a_other, place, count, rows)
    assemble(fb, b_own, b_other, place, count, rows)
    even = place[2] == 0
    half = KV_WIDTH // PARTS
    gk = jnp.concatenate([g[:, :half] for g in grads], axis=1)
    gv = jnp.concatenate([g[:, half:] for g in grads], axis=1)
    ga = jnp.where(even, gk, gv)
    gb = jnp.where(even, gv, gk)
    out[...] = (nt(ga, fa[...]) + nt(gb, fb[...])).astype(jnp.bfloat16)


def input_grad_of(place, grads, a_own, a_other, b_own, b_other, count, rows):
    full = pltpu.VMEM((2 * count * rows, KV_WIDTH), jnp.bfloat16)
    return pl.pallas_call(
        functools.partial(input_grad_kernel, count=count, rows=rows),
        in_specs=[sspec()] + [vspec()] * (4 + len(grads)),
        out_specs=vspec(),
        out_shape=jax.ShapeDtypeStruct((grads[0].shape[0], 2 * count * rows), jnp.bfloat16),
        scratch_shapes=[full, full],
        compiler_params=params(),
        name="input_grad",
    )(place, *grads, a_own, a_other, b_own, b_other)


def turn_kernel(place, here, *refs, count, rows):
    wrapped, returned, out = refs[: count - 1], refs[count - 1 : 2 * count - 2], refs[-1]
    block = here.shape[0]
    for k in range(count):
        if k == 0:
            got = here[...]
        else:
            got = jnp.where(place[0] >= k, returned[count - k - 1][...], wrapped[k - 1][:block, :])
        for core in range(2):
            at = (2 * k + core) * block
            out[:, at : at + block] = got[:, core * rows : (core + 1) * rows].T


def turn(place, here, wrapped, returned, rows):
    count = len(wrapped) + 1
    return pl.pallas_call(
        functools.partial(turn_kernel, count=count, rows=rows),
        in_specs=[sspec()] + [vspec()] * (2 * count - 1),
        out_specs=vspec(),
        out_shape=jax.ShapeDtypeStruct((rows, 2 * count * here.shape[0]), here.dtype),
        compiler_params=params(),
        name="turn",
    )(place, here, *wrapped, *returned)


def weight_grad_kernel(x_turned, g_own, g_other, out, *, count):
    size = g_own.shape[0] // count
    pieces = []
    for k in range(count):
        pieces += [g_own[k * size : (k + 1) * size, :], g_other[k * size : (k + 1) * size, :]]
    grads = jnp.concatenate(pieces, axis=0)
    out[...] = jnp.dot(x_turned[...], grads, preferred_element_type=jnp.float32).astype(jnp.bfloat16)


def weight_grad_of(x_turned, g_own, g_other, count):
    return pl.pallas_call(
        functools.partial(weight_grad_kernel, count=count),
        in_specs=[vspec()] * 3,
        out_specs=vspec(),
        out_shape=jax.ShapeDtypeStruct((x_turned.shape[0], g_own.shape[1]), jnp.bfloat16),
        compiler_params=params(),
        name="weight_grad",
    )(x_turned, g_own, g_other)


def finish_kernel(*refs):
    pairs, outs = refs[:-2], refs[-2:]
    half = KV_WIDTH // PARTS
    for part in range(PARTS):
        a, b = pairs[2 * part], pairs[2 * part + 1]
        grad = (a[...].astype(jnp.float32) + b[...].astype(jnp.float32)).astype(jnp.bfloat16)
        outs[0][:, part * half : (part + 1) * half] = grad[:, :half]
        outs[1][:, part * half : (part + 1) * half] = grad[:, half:]


def finish(*partials):
    out = jax.ShapeDtypeStruct((partials[0].shape[0], KV_WIDTH), jnp.bfloat16)
    return pl.pallas_call(
        finish_kernel,
        in_specs=[vspec()] * len(partials),
        out_specs=[vspec()] * 2,
        out_shape=[out, out],
        compiler_params=params(),
        name="finish",
    )(*partials)


def body(activations, queries, key_weight, value_weight, segment_ids, out_grad):
    inputs = activations[0]
    block, width = inputs.shape
    rows = key_weight.shape[0]
    n = lax.axis_size("seq")
    reps = lax.axis_size("rep")
    z, r, c = lax.axis_index("seq"), lax.axis_index("rep"), lax.axis_index("fsdp")
    odd = lax.rem(r, 2)
    place = jnp.stack([z, c, odd]).astype(jnp.int32)
    shifts = range(1, n)

    def around(x, k):
        return lax.ppermute(x, "seq", [(i, (i + k) % n) for i in range(n)])

    def up(x, k):
        return lax.ppermute(x, "seq", [(i, i + k) for i in range(n - k)])

    def down(x, k):
        return lax.ppermute(x, "seq", [(i, i - k) for i in range(k, n)])

    def partner(x):
        return lax.ppermute(x, "rep", [(j, j ^ 1) for j in range(reps)])

    def core(x):
        return lax.ppermute(x, "fsdp", [(0, 1), (1, 0)])

    half = jnp.where(odd == 0, key_weight, value_weight)
    gathered = [half] + [around(half, k) for k in shifts]
    x_next = partner(inputs)

    late, gathered[1] = lax.optimization_barrier((inputs, gathered[1]))
    columns = late.reshape(block, n, 2, rows)
    x_mine = lax.dynamic_index_in_dim(columns, c, 2, keepdims=False)
    x_theirs = core(lax.dynamic_index_in_dim(columns, 1 - c, 2, keepdims=False))
    x_both = jnp.concatenate([x_mine, x_theirs], axis=2).transpose(1, 0, 2)
    x_both = jnp.pad(x_both, ((0, 0), (0, 0), (0, KV_WIDTH - 2 * rows)))
    x_for = [
        lax.dynamic_index_in_dim(x_both, lax.rem(z + k, n), 0, keepdims=False) for k in range(n)
    ]
    gathered, x_next, x_for = lax.optimization_barrier((gathered, x_next, x_for))

    w_own = jnp.concatenate(gathered, axis=0)
    w_other = core(w_own)
    own, other = project(place, segment_ids, inputs, x_next, w_own, w_other, n, rows)
    pair_a, pair_b, loads = pack(place, own, partner(other), x_for[1:])
    carried = [around(x, k) for k, x in zip(shifts, loads)]
    pairs = [[pair_a] + carried, [pair_b] + [up(pair_b, k) for k in shifts]]

    w_late, _ = lax.optimization_barrier((w_own, carried[0]))
    b_own = partner(w_late)
    b_other = core(b_own)

    before, sums = [], []
    for part in range(PARTS):
        before, sent, total = attend(
            place, queries[0], out_grad[0], pairs[part], part, x_for[:0:-1], before
        )
        if part == 0:
            back = [around(x, n - k) for k, x in zip(shifts, sent)]
            returned = back
            back = [jnp.where(z + k < n, x, jnp.zeros_like(x)) for k, x in zip(shifts, back)]
        else:
            back = [down(x, k) for k, x in zip(shifts, sent)]
        for x in back:
            total = total + x.astype(jnp.float32)
        sums.append(total.astype(jnp.bfloat16))
    context, query_grad = before[:2]
    x_turned = turn(place, x_for[0], carried, returned, rows)

    input_grad = input_grad_of(place, sums, w_own, w_other, b_own, b_other, n, rows)
    partials = []
    for part in range(PARTS):
        g_own = jnp.concatenate([sums[part]] + [around(sums[part], k) for k in shifts], axis=0)
        g_other = core(g_own)
        if part == PARTS - 1:
            g_other, input_grad = lax.optimization_barrier((g_other, input_grad))
        partials.append(weight_grad_of(x_turned, g_own, g_other, n))
    if reps == 2:
        grads = finish(*[x for p in partials for x in (p, partner(p))])
    else:
        totals = [lax.psum(p.astype(jnp.float32), "rep").astype(jnp.bfloat16) for p in partials]
        grads = finish(*[x for p in totals for x in (p, jnp.zeros_like(p))])
    return context[None], query_grad[None], input_grad[None], grads[0], grads[1]


def solution(mesh):
    return jax.shard_map(
        body,
        mesh=mesh,
        in_specs=(
            P(("groups", "rep", "fsdp"), "seq", None),
            P(("groups", "rep", "fsdp"), "seq", None),
            P(("seq", "fsdp"), None),
            P(("seq", "fsdp"), None),
            P(("groups", "rep", "fsdp"), "seq"),
            P(("groups", "rep", "fsdp"), "seq", None),
        ),
        out_specs=(
            P(("groups", "rep", "fsdp"), "seq", None),
            P(("groups", "rep", "fsdp"), "seq", None),
            P(("groups", "rep", "fsdp"), "seq", None),
            P(("groups", "seq", "fsdp"), None),
            P(("groups", "seq", "fsdp"), None),
        ),
        check_vma=False,
    )
```

```python
import functools
import math

import jax
import jax.numpy as jnp
from jax import lax
from jax.experimental import pallas as pl
from jax.experimental.pallas import tpu as pltpu
from jax.sharding import PartitionSpec as P

HEADS = 16
KV_HEADS = 4
HEAD_DIM = 128
KV_WIDTH = KV_HEADS * HEAD_DIM
GROUP = HEADS // KV_HEADS
PARTS = 2
LOG2E = 1.4426950408889634
MASKED = -1e30
EXTRA = 16
VMEM_LIMIT = 56 * 1024 * 1024


def params(**kw):
    return pltpu.CompilerParams(vmem_limit_bytes=VMEM_LIMIT, **kw)


def vspec():
    return pl.BlockSpec(memory_space=pltpu.VMEM)


def sspec():
    return pl.BlockSpec(memory_space=pltpu.SMEM)


def assemble(full_ref, own_ref, other_ref, place, count, rows):
    z, c = place[0], place[1]
    for k in range(count):
        src = lax.rem(z - k + count, count)
        for ref, core in ((own_ref, c), (other_ref, 1 - c)):
            start = pl.multiple_of((src * 2 + core) * rows, rows)
            full_ref[pl.ds(start, rows), :] = ref[k * rows : (k + 1) * rows, :]


def project_kernel(
    place, seg, x_own, x_next, w_own, w_other, out_own, out_next, full, *, count, rows
):
    assemble(full, w_own, w_other, place, count, rows)
    w = full[...]
    block = x_own.shape[0]
    out_own[:block, :] = jnp.dot(x_own[...], w, preferred_element_type=jnp.float32).astype(
        jnp.bfloat16
    )
    ids = (seg[...] + 1).astype(jnp.float32)
    wide = jnp.concatenate([jnp.broadcast_to(ids, (EXTRA, block))] * (KV_WIDTH // block), axis=1)
    out_own[block:, :] = wide.astype(jnp.bfloat16)
    out_next[...] = jnp.dot(x_next[...], w, preferred_element_type=jnp.float32).astype(jnp.bfloat16)


def project(place, seg, x_own, x_next, w_own, w_other, count, rows):
    width = w_own.shape[1]
    block = x_own.shape[0]
    return pl.pallas_call(
        functools.partial(project_kernel, count=count, rows=rows),
        in_specs=[sspec()] + [vspec()] * 5,
        out_specs=[vspec()] * 2,
        out_shape=[
            jax.ShapeDtypeStruct((block + EXTRA, width), jnp.bfloat16),
            jax.ShapeDtypeStruct((block, width), jnp.bfloat16),
        ],
        scratch_shapes=[pltpu.VMEM((2 * count * rows, width), jnp.bfloat16)],
        compiler_params=params(),
        name="project",
    )(place, seg, x_own, x_next, w_own, w_other)


def pack_kernel(place, own, mate, *refs, count):
    cols, outs = refs[: count - 1], refs[count - 1 :]
    block, width = mate.shape
    half = width // PARTS
    first = jnp.concatenate([own[:block, :half], mate[:, :half]], axis=1)
    tail = own[block:, :]
    outs[0][:block, :] = first
    outs[0][block:, :] = tail
    outs[1][...] = jnp.concatenate([own[:block, half:], mate[:, half:]], axis=1)
    for k in range(1, count):
        goes_up = place[0] + k < count
        outs[k + 1][:block, :] = jnp.where(goes_up, first, cols[k - 1][...])
        outs[k + 1][block:, :] = jnp.where(goes_up, tail, jnp.zeros_like(tail))


def pack(place, own, mate, cols):
    count = len(cols) + 1
    tall = jax.ShapeDtypeStruct(own.shape, own.dtype)
    outs = pl.pallas_call(
        functools.partial(pack_kernel, count=count),
        in_specs=[sspec()] + [vspec()] * (count + 1),
        out_specs=[vspec()] * (count + 1),
        out_shape=[tall, jax.ShapeDtypeStruct(mate.shape, mate.dtype)] + [tall] * (count - 1),
        compiler_params=params(),
        name="pack",
    )(place, own, mate, *cols)
    return outs[0], outs[1], outs[2:]


def nt(a, b):
    return lax.dot_general(a, b, (((1,), (1,)), ((), ())), preferred_element_type=jnp.float32)


def tn(a, b):
    return lax.dot_general(a, b, (((0,), (0,)), ((), ())), preferred_element_type=jnp.float32)


def attend_kernel(place, q_ref, do_ref, *refs, count, block, opening):
    first, second = refs[:count], refs[count : 2 * count]
    refs = refs[2 * count :]
    if opening:
        seg_refs, cols = refs[:count], refs[count : 2 * count - 1]
        ctx_ref, dq_ref, bias = refs[2 * count - 1 : 2 * count + 2]
        grads, own_grad = refs[2 * count + 2 : 3 * count + 1], refs[-1]
    else:
        bias = refs[0]
        ctx_ref, dq_ref = refs[3:5]
        grads, own_grad = refs[5:-1], refs[-1]
    inv_root = 1.0 / math.sqrt(HEAD_DIM)
    length = count * block

    if opening:

        @pl.when(pl.program_id(0) == 0)
        def _():
            ids = [r[:1, :].astype(jnp.float32) for r in seg_refs]
            mine = jnp.broadcast_to(ids[0], (block, block)).T
            rows = lax.broadcasted_iota(jnp.int32, (block, block), 0)
            cols_here = lax.broadcasted_iota(jnp.int32, (block, block), 1)
            for k in range(count):
                ok = mine == jnp.broadcast_to(ids[k], (block, block))
                if k == 0:
                    ok = ok & (cols_here <= rows)
                bias[:, k * block : (k + 1) * block] = jnp.where(ok, 0.0, MASKED)

    even = place[2] == 0
    a = jnp.concatenate([r[...] for r in first], axis=0)
    b = jnp.concatenate([r[...] for r in second], axis=0)
    key = jnp.where(even, a, b)
    value = jnp.where(even, b, a)

    def stack(ref):
        return jnp.concatenate(
            [ref[:, h * HEAD_DIM : (h + 1) * HEAD_DIM] for h in range(GROUP)], axis=0
        )

    def unstack(ref, val):
        for h in range(GROUP):
            ref[:, h * HEAD_DIM : (h + 1) * HEAD_DIM] = val[h * block : (h + 1) * block, :]

    q, do = stack(q_ref), stack(do_ref)
    s = nt(q, key) * (inv_root * LOG2E)
    s = (s.reshape(GROUP, block, length) + bias[...][None]).reshape(GROUP * block, length)
    e = jnp.exp2(s - jnp.max(s, axis=1, keepdims=True))
    p = e * (1.0 / jnp.sum(e, axis=1, keepdims=True))
    p_low = p.astype(jnp.bfloat16)
    ctx = jnp.dot(p_low, value, preferred_element_type=jnp.float32).astype(jnp.bfloat16)
    unstack(ctx_ref, ctx)
    dots = jnp.sum(do.astype(jnp.float32) * ctx.astype(jnp.float32), axis=1, keepdims=True)
    ds = (p * (nt(do, value) - dots)).astype(jnp.bfloat16)
    dq = jnp.dot(ds, key, preferred_element_type=jnp.float32) * inv_root
    unstack(dq_ref, dq.astype(jnp.bfloat16))
    dv = tn(p_low, do)
    dk = tn(ds, q) * inv_root
    at_key = pl.multiple_of(pl.program_id(0) * HEAD_DIM, HEAD_DIM)
    at_value = pl.multiple_of(at_key + KV_WIDTH // PARTS, HEAD_DIM)
    own_grad[:, pl.ds(at_key, HEAD_DIM)] = dk[:block]
    own_grad[:, pl.ds(at_value, HEAD_DIM)] = dv[:block]
    for k in range(1, count):
        piece = slice(k * block, (k + 1) * block)
        for at, grad in ((at_key, dk), (at_value, dv)):
            sent = grad[piece].astype(jnp.bfloat16)
            if opening:
                sent = jnp.where(place[0] >= k, sent, cols[k - 1][:, pl.ds(at, HEAD_DIM)])
            grads[k - 1][:, pl.ds(at, HEAD_DIM)] = sent


def attend(place, q, do, pairs, part, cols, before):
    block, width = q.shape
    count = len(pairs)
    steps = KV_HEADS // PARTS
    opening = not before
    wide = pl.BlockSpec((block, GROUP * HEAD_DIM), lambda g: (0, part * steps + g))
    first = pl.BlockSpec((block, HEAD_DIM), lambda g: (0, g))
    second = pl.BlockSpec((block, HEAD_DIM), lambda g: (0, steps + g))
    both = 2 * KV_WIDTH // PARTS
    held = pl.BlockSpec((block, both), lambda g: (0, 0))
    bias = pl.BlockSpec((block, count * block), lambda g: (0, 0))
    seg = pl.BlockSpec((EXTRA, block), lambda g: (block // EXTRA, 0))
    rows = jax.ShapeDtypeStruct((block, width), jnp.bfloat16)
    own = jax.ShapeDtypeStruct((block, both), jnp.float32)
    sent = jax.ShapeDtypeStruct((block, both), jnp.bfloat16)
    operands = [place, q, do, *pairs, *pairs]
    in_specs = [sspec(), wide, wide] + [first] * count + [second] * count
    if opening:
        operands += [*pairs, *cols]
        in_specs += [seg] * count + [held] * (count - 1)
        out_specs = [wide, wide, bias] + [held] * count
        out_shape = [rows, rows, jax.ShapeDtypeStruct((block, count * block), jnp.float32)]
        aliases = {}
    else:
        context, query_grad, mask = before
        aliases = {len(operands) + 1: 0, len(operands) + 2: 1}
        operands += [mask, context, query_grad]
        in_specs += [bias] + [pl.BlockSpec(memory_space=pl.ANY)] * 2
        out_specs = [wide, wide] + [held] * count
        out_shape = [rows, rows]
    outs = pl.pallas_call(
        functools.partial(attend_kernel, count=count, block=block, opening=opening),
        grid=(steps,),
        in_specs=in_specs,
        out_specs=out_specs,
        out_shape=out_shape + [sent] * (count - 1) + [own],
        input_output_aliases=aliases,
        compiler_params=params(dimension_semantics=("arbitrary",)),
        name="attend",
    )(*operands)
    return outs[: len(outs) - count], outs[len(outs) - count : -1], outs[-1]


def input_grad_kernel(place, *refs, count, rows):
    grads = refs[:PARTS]
    a_own, a_other, b_own, b_other, out, fa, fb = refs[PARTS:]
    assemble(fa, a_own, a_other, place, count, rows)
    assemble(fb, b_own, b_other, place, count, rows)
    even = place[2] == 0
    half = KV_WIDTH // PARTS
    gk = jnp.concatenate([g[:, :half] for g in grads], axis=1)
    gv = jnp.concatenate([g[:, half:] for g in grads], axis=1)
    ga = jnp.where(even, gk, gv)
    gb = jnp.where(even, gv, gk)
    out[...] = (nt(ga, fa[...]) + nt(gb, fb[...])).astype(jnp.bfloat16)


def input_grad_of(place, grads, a_own, a_other, b_own, b_other, count, rows):
    full = pltpu.VMEM((2 * count * rows, KV_WIDTH), jnp.bfloat16)
    return pl.pallas_call(
        functools.partial(input_grad_kernel, count=count, rows=rows),
        in_specs=[sspec()] + [vspec()] * (4 + len(grads)),
        out_specs=vspec(),
        out_shape=jax.ShapeDtypeStruct((grads[0].shape[0], 2 * count * rows), jnp.bfloat16),
        scratch_shapes=[full, full],
        compiler_params=params(),
        name="input_grad",
    )(place, *grads, a_own, a_other, b_own, b_other)


def turn_kernel(place, here, *refs, count, rows):
    wrapped, returned, out = refs[: count - 1], refs[count - 1 : 2 * count - 2], refs[-1]
    block = here.shape[0]
    for k in range(count):
        if k == 0:
            got = here[...]
        else:
            got = jnp.where(place[0] >= k, returned[count - k - 1][...], wrapped[k - 1][:block, :])
        for core in range(2):
            at = (2 * k + core) * block
            out[:, at : at + block] = got[:, core * rows : (core + 1) * rows].T


def turn(place, here, wrapped, returned, rows):
    count = len(wrapped) + 1
    return pl.pallas_call(
        functools.partial(turn_kernel, count=count, rows=rows),
        in_specs=[sspec()] + [vspec()] * (2 * count - 1),
        out_specs=vspec(),
        out_shape=jax.ShapeDtypeStruct((rows, 2 * count * here.shape[0]), here.dtype),
        compiler_params=params(),
        name="turn",
    )(place, here, *wrapped, *returned)


def weight_grad_kernel(x_turned, g_own, g_other, out, *, count):
    size = g_own.shape[0] // count
    pieces = []
    for k in range(count):
        pieces += [g_own[k * size : (k + 1) * size, :], g_other[k * size : (k + 1) * size, :]]
    grads = jnp.concatenate(pieces, axis=0)
    out[...] = jnp.dot(x_turned[...], grads, preferred_element_type=jnp.float32).astype(jnp.bfloat16)


def weight_grad_of(x_turned, g_own, g_other, count):
    return pl.pallas_call(
        functools.partial(weight_grad_kernel, count=count),
        in_specs=[vspec()] * 3,
        out_specs=vspec(),
        out_shape=jax.ShapeDtypeStruct((x_turned.shape[0], g_own.shape[1]), jnp.bfloat16),
        compiler_params=params(),
        name="weight_grad",
    )(x_turned, g_own, g_other)


def finish_kernel(*refs):
    pairs, outs = refs[:-2], refs[-2:]
    half = KV_WIDTH // PARTS
    for part in range(PARTS):
        a, b = pairs[2 * part], pairs[2 * part + 1]
        grad = (a[...].astype(jnp.float32) + b[...].astype(jnp.float32)).astype(jnp.bfloat16)
        outs[0][:, part * half : (part + 1) * half] = grad[:, :half]
        outs[1][:, part * half : (part + 1) * half] = grad[:, half:]


def finish(*partials):
    out = jax.ShapeDtypeStruct((partials[0].shape[0], KV_WIDTH), jnp.bfloat16)
    return pl.pallas_call(
        finish_kernel,
        in_specs=[vspec()] * len(partials),
        out_specs=[vspec()] * 2,
        out_shape=[out, out],
        compiler_params=params(),
        name="finish",
    )(*partials)


def body(activations, queries, key_weight, value_weight, segment_ids, out_grad):
    inputs = activations[0]
    block, width = inputs.shape
    rows = key_weight.shape[0]
    n = lax.axis_size("seq")
    reps = lax.axis_size("rep")
    z, r, c = lax.axis_index("seq"), lax.axis_index("rep"), lax.axis_index("fsdp")
    odd = lax.rem(r, 2)
    place = jnp.stack([z, c, odd]).astype(jnp.int32)
    shifts = range(1, n)

    def around(x, k):
        return lax.ppermute(x, "seq", [(i, (i + k) % n) for i in range(n)])

    def up(x, k):
        return lax.ppermute(x, "seq", [(i, i + k) for i in range(n - k)])

    def down(x, k):
        return lax.ppermute(x, "seq", [(i, i - k) for i in range(k, n)])

    def partner(x):
        return lax.ppermute(x, "rep", [(j, j ^ 1) for j in range(reps)])

    def core(x):
        return lax.ppermute(x, "fsdp", [(0, 1), (1, 0)])

    half = jnp.where(odd == 0, key_weight, value_weight)
    gathered = [half] + [around(half, k) for k in shifts]
    x_next = partner(inputs)

    late, gathered[1] = lax.optimization_barrier((inputs, gathered[1]))
    columns = late.reshape(block, n, 2, rows)
    x_mine = lax.dynamic_index_in_dim(columns, c, 2, keepdims=False)
    x_theirs = core(lax.dynamic_index_in_dim(columns, 1 - c, 2, keepdims=False))
    x_both = jnp.concatenate([x_mine, x_theirs], axis=2).transpose(1, 0, 2)
    x_both = jnp.pad(x_both, ((0, 0), (0, 0), (0, KV_WIDTH - 2 * rows)))
    x_for = [
        lax.dynamic_index_in_dim(x_both, lax.rem(z + k, n), 0, keepdims=False) for k in range(n)
    ]
    gathered, x_next, x_for = lax.optimization_barrier((gathered, x_next, x_for))

    w_own = jnp.concatenate(gathered, axis=0)
    w_other = core(w_own)
    own, other = project(place, segment_ids, inputs, x_next, w_own, w_other, n, rows)
    pair_a, pair_b, loads = pack(place, own, partner(other), x_for[1:])
    carried = [around(x, k) for k, x in zip(shifts, loads)]
    pairs = [[pair_a] + carried, [pair_b] + [up(pair_b, k) for k in shifts]]

    queries, out_grad = queries[0], out_grad[0]
    before, sent_a, own_a = attend(place, queries, out_grad, pairs[0], 0, x_for[:0:-1], [])
    returned = [around(x, n - k) for k, x in zip(shifts, sent_a)]
    before, sent_b, own_b = attend(place, queries, out_grad, pairs[1], 1, [], before)
    back_b = [down(x, k) for k, x in zip(shifts, sent_b)]
    returned, _ = lax.optimization_barrier((returned, sent_b))
    back_a = [jnp.where(z + k < n, x, jnp.zeros_like(x)) for k, x in zip(shifts, returned)]
    sums = []
    for total, back in ((own_a, back_a), (own_b, back_b)):
        for x in back:
            total = total + x.astype(jnp.float32)
        sums.append(total.astype(jnp.bfloat16))
    context, query_grad = before[:2]
    x_turned = turn(place, x_for[0], carried, returned, rows)

    w_late, _ = lax.optimization_barrier((w_own, sums[1]))
    b_own = partner(w_late)
    b_other = core(b_own)
    partials = []
    for part in range(PARTS):
        pieces = [sums[part]] + [around(sums[part], k) for k in shifts]
        if part == 0:
            pieces, _ = lax.optimization_barrier((pieces, sums[1]))
        if part == PARTS - 1:
            pieces, partials = lax.optimization_barrier((pieces, partials))
        g_own = jnp.concatenate(pieces, axis=0)
        partials.append(weight_grad_of(x_turned, g_own, core(g_own), n))
    sums, _ = lax.optimization_barrier((sums, partials[-1]))
    input_grad = input_grad_of(place, sums, w_own, w_other, b_own, b_other, n, rows)
    if reps == 2:
        others = [partner(p) for p in partials]
        others, input_grad = lax.optimization_barrier((others, input_grad))
        grads = finish(*[x for p in zip(partials, others) for x in p])
    else:
        totals = [lax.psum(p.astype(jnp.float32), "rep").astype(jnp.bfloat16) for p in partials]
        grads = finish(*[x for p in totals for x in (p, jnp.zeros_like(p))])
    return context[None], query_grad[None], input_grad[None], grads[0], grads[1]


def solution(mesh):
    return jax.shard_map(
        body,
        mesh=mesh,
        in_specs=(
            P(("groups", "rep", "fsdp"), "seq", None),
            P(("groups", "rep", "fsdp"), "seq", None),
            P(("seq", "fsdp"), None),
            P(("seq", "fsdp"), None),
            P(("groups", "rep", "fsdp"), "seq"),
            P(("groups", "rep", "fsdp"), "seq", None),
        ),
        out_specs=(
            P(("groups", "rep", "fsdp"), "seq", None),
            P(("groups", "rep", "fsdp"), "seq", None),
            P(("groups", "rep", "fsdp"), "seq", None),
            P(("groups", "seq", "fsdp"), None),
            P(("groups", "seq", "fsdp"), None),
        ),
        check_vma=False,
    )
```

```python
import functools
import math

import jax
import jax.numpy as jnp
from jax import lax
from jax.experimental import pallas as pl
from jax.experimental.pallas import tpu as pltpu
from jax.sharding import PartitionSpec as P

HEADS = 16
KV_HEADS = 4
HEAD_DIM = 128
KV_WIDTH = KV_HEADS * HEAD_DIM
GROUP = HEADS // KV_HEADS
PARTS = 2
LOG2E = 1.4426950408889634
MASKED = -1e30
EXTRA = 16
MIB = 1024 * 1024


def params(mib=16, **kw):
    return pltpu.CompilerParams(vmem_limit_bytes=mib * MIB, **kw)


def vspec():
    return pl.BlockSpec(memory_space=pltpu.VMEM)


def near(*xs):
    return [pltpu.with_memory_space_constraint(x, pltpu.VMEM) for x in xs]


def sspec():
    return pl.BlockSpec(memory_space=pltpu.SMEM)


def assemble(full_ref, own_ref, other_ref, place, count, rows, left=0):
    z, c = place[0], place[1]
    right = left + own_ref.shape[1]
    for k in range(count):
        src = lax.rem(z - k + count, count)
        for ref, core in ((own_ref, c), (other_ref, 1 - c)):
            start = pl.multiple_of((src * 2 + core) * rows, rows)
            full_ref[pl.ds(start, rows), left:right] = ref[k * rows : (k + 1) * rows, :]


def project_kernel(place, seg, x_own, x_next, w_own, w_other, out_own, out_next, full, *, count, rows):
    assemble(full, w_own, w_other, place, count, rows)
    w = full[...]
    block = x_own.shape[0]
    out_next[...] = jnp.dot(x_next[...], w, preferred_element_type=jnp.float32).astype(jnp.bfloat16)
    out_own[:block, :] = jnp.dot(x_own[...], w, preferred_element_type=jnp.float32).astype(
        jnp.bfloat16
    )
    ids = (seg[...] + 1).astype(jnp.float32)
    copies = out_own.shape[1] // block
    wide = jnp.concatenate([jnp.broadcast_to(ids, (EXTRA, block))] * copies, axis=1)
    out_own[block:, :] = wide.astype(jnp.bfloat16)


def project(place, seg, x_own, x_next, w_own, w_other, count, rows):
    width = w_own.shape[1]
    block = x_own.shape[0]
    return pl.pallas_call(
        functools.partial(project_kernel, count=count, rows=rows),
        in_specs=[sspec()] + [vspec()] * 5,
        out_specs=[vspec()] * 2,
        out_shape=[
            pltpu.VMEM((block + EXTRA, width), jnp.bfloat16),
            pltpu.VMEM((block, width), jnp.bfloat16),
        ],
        scratch_shapes=[pltpu.VMEM((2 * count * rows, width), jnp.bfloat16)],
        compiler_params=params(),
        name="project",
    )(place, seg, x_own, *near(x_next, w_own, w_other))


def cut_kernel(place, own, other, *outs, count, rows):
    for k in range(count):
        start = (lax.rem(place[0] + k, count) * 2 + place[1]) * rows
        start = pl.multiple_of(start, rows)
        outs[k][:, :rows] = own[:, pl.ds(start, rows)]
        outs[k][:, rows:] = other[:, pl.ds(start, rows)]


def cut(place, own, other, count, rows):
    block = own.shape[0]
    if rows % 128 or 2 * rows != KV_WIDTH:
        pieces = []
        for k in range(count):
            start = (lax.rem(place[0] + k, count) * 2 + place[1]) * rows
            both = [lax.dynamic_slice_in_dim(x, start, rows, 1) for x in (own, other)]
            wide = jnp.concatenate(both, axis=1)
            pieces.append(jnp.pad(wide, ((0, 0), (0, KV_WIDTH - 2 * rows))))
        return pieces
    return pl.pallas_call(
        functools.partial(cut_kernel, count=count, rows=rows),
        in_specs=[sspec()] + [vspec()] * 2,
        out_specs=[vspec()] * count,
        out_shape=[pltpu.VMEM((block, 2 * rows), own.dtype)] * count,
        compiler_params=params(),
        name="cut",
    )(place, own, *near(other))


def pack_kernel(place, own, mate, *refs, count):
    cols, outs = refs[: count - 1], refs[count - 1 :]
    block, half = mate.shape
    first = jnp.concatenate([own[:block, :], mate[...]], axis=1)
    tail = own[block:, :]
    outs[0][:block, :] = first
    outs[0][block:, :half] = tail
    outs[0][block:, half:] = jnp.zeros_like(tail)
    for k in range(1, count):
        goes_up = place[0] + k < count
        outs[k][:block, :] = jnp.where(goes_up, first, cols[k - 1][...])
        outs[k][block:, :half] = jnp.where(goes_up, tail, jnp.zeros_like(tail))
        outs[k][block:, half:] = jnp.zeros_like(tail)


def pack(place, own, mate, cols):
    count = len(cols) + 1
    tall = pltpu.VMEM((own.shape[0], 2 * own.shape[1]), own.dtype)
    outs = pl.pallas_call(
        functools.partial(pack_kernel, count=count),
        in_specs=[sspec()] + [vspec()] * (count + 1),
        out_specs=[vspec()] * count,
        out_shape=[tall] * count,
        compiler_params=params(),
        name="pack",
    )(place, *near(own, mate, *cols))
    return outs[0], outs[1:]


def nt(a, b):
    return lax.dot_general(a, b, (((1,), (1,)), ((), ())), preferred_element_type=jnp.float32)


def tn(a, b):
    return lax.dot_general(a, b, (((0,), (0,)), ((), ())), preferred_element_type=jnp.float32)


def attend_kernel(place, q_ref, do_ref, *refs, count, block, opening):
    pair_refs, refs = refs[:count], refs[count:]
    if opening:
        cols = refs[: count - 1]
        ctx_ref, dq_ref, bias = refs[count - 1 : count + 2]
        grads, own_grad = refs[count + 2 : -1], refs[-1]
    else:
        bias = refs[0]
        ctx_ref, dq_ref = refs[3:5]
        grads, own_grad = refs[5:-1], refs[-1]
    inv_root = 1.0 / math.sqrt(HEAD_DIM)
    length = count * block

    if opening:

        @pl.when(pl.program_id(0) == 0)
        def _():
            ids = [r[block : block + 1, :block].astype(jnp.float32) for r in pair_refs]
            mine = jnp.broadcast_to(ids[0], (block, block)).T
            rows = lax.broadcasted_iota(jnp.int32, (block, block), 0)
            cols_here = lax.broadcasted_iota(jnp.int32, (block, block), 1)
            for k in range(count):
                ok = mine == jnp.broadcast_to(ids[k], (block, block))
                if k == 0:
                    ok = ok & (cols_here <= rows)
                bias[:, k * block : (k + 1) * block] = jnp.where(ok, 0.0, MASKED)

    even = place[2] == 0
    at_key = pl.multiple_of(pl.program_id(0) * HEAD_DIM, HEAD_DIM)
    at_value = pl.multiple_of(at_key + KV_WIDTH // PARTS, HEAD_DIM)
    a = jnp.concatenate([r[:block, pl.ds(at_key, HEAD_DIM)] for r in pair_refs], axis=0)
    b = jnp.concatenate([r[:block, pl.ds(at_value, HEAD_DIM)] for r in pair_refs], axis=0)
    key = jnp.where(even, a, b)
    value = jnp.where(even, b, a)

    def stack(ref):
        return jnp.concatenate(
            [ref[:, h * HEAD_DIM : (h + 1) * HEAD_DIM] for h in range(GROUP)], axis=0
        )

    def unstack(ref, val):
        for h in range(GROUP):
            ref[:, h * HEAD_DIM : (h + 1) * HEAD_DIM] = val[h * block : (h + 1) * block, :]

    q, do = stack(q_ref), stack(do_ref)
    s = nt(q, key) * (inv_root * LOG2E)
    s = (s.reshape(GROUP, block, length) + bias[...][None]).reshape(GROUP * block, length)
    e = jnp.exp2(s - jnp.max(s, axis=1, keepdims=True))
    p = e * (1.0 / jnp.sum(e, axis=1, keepdims=True))
    p_low = p.astype(jnp.bfloat16)
    ctx = jnp.dot(p_low, value, preferred_element_type=jnp.float32).astype(jnp.bfloat16)
    unstack(ctx_ref, ctx)
    dots = jnp.sum(do.astype(jnp.float32) * ctx.astype(jnp.float32), axis=1, keepdims=True)
    ds = (p * (nt(do, value) - dots)).astype(jnp.bfloat16)
    dq = jnp.dot(ds, key, preferred_element_type=jnp.float32) * inv_root
    unstack(dq_ref, dq.astype(jnp.bfloat16))
    dv = tn(p_low, do)
    dk = tn(ds, q) * inv_root
    own_grad[:, pl.ds(at_key, HEAD_DIM)] = dk[:block]
    own_grad[:, pl.ds(at_value, HEAD_DIM)] = dv[:block]
    for k in range(1, count):
        piece = slice(k * block, (k + 1) * block)
        for at, grad in ((at_key, dk), (at_value, dv)):
            sent = grad[piece].astype(jnp.bfloat16)
            if opening:
                sent = jnp.where(place[0] >= k, sent, cols[k - 1][:, pl.ds(at, HEAD_DIM)])
            grads[k - 1][:, pl.ds(at, HEAD_DIM)] = sent


def attend(place, q, do, pairs, part, cols, before):
    block, width = q.shape
    count = len(pairs)
    steps = KV_HEADS // PARTS
    opening = not before

    def at_part(g, place):
        return (0, (place[3] if part == 0 else 1 - place[3]) * steps + g)

    wide = pl.BlockSpec((block, GROUP * HEAD_DIM), at_part)
    both = 2 * KV_WIDTH // PARTS
    rows = jax.ShapeDtypeStruct((block, width), jnp.bfloat16)
    own = jax.ShapeDtypeStruct((block, both), jnp.float32)
    sent = pltpu.VMEM((block, both), jnp.bfloat16)
    operands = [place, q, do, *near(*pairs)]
    in_specs = [wide, wide] + [vspec()] * count
    if opening:
        operands += near(*cols)
        in_specs += [vspec()] * (count - 1)
        out_specs = [wide, wide, vspec()] + [vspec()] * count
        out_shape = [rows, rows, jax.ShapeDtypeStruct((block, count * block), jnp.float32)]
        aliases = {}
    else:
        context, query_grad, mask = before
        aliases = {len(operands) + 1: 0, len(operands) + 2: 1}
        operands += [mask, context, query_grad]
        in_specs += [vspec()] + [pl.BlockSpec(memory_space=pl.ANY)] * 2
        out_specs = [wide, wide] + [vspec()] * count
        out_shape = [rows, rows]
    outs = pl.pallas_call(
        functools.partial(attend_kernel, count=count, block=block, opening=opening),
        grid_spec=pltpu.PrefetchScalarGridSpec(
            num_scalar_prefetch=1, grid=(steps,), in_specs=in_specs, out_specs=out_specs
        ),
        out_shape=out_shape + [sent] * (count - 1) + [own],
        input_output_aliases=aliases,
        compiler_params=params(4 + 3 * count, dimension_semantics=("arbitrary",)),
        name="attend",
    )(*operands)
    return outs[: len(outs) - count], outs[len(outs) - count : -1], outs[-1]


def input_grad_kernel(place, *refs, count, rows):
    grads = refs[:PARTS]
    own = refs[PARTS : 3 * PARTS]
    late, (out, fa, fb) = refs[3 * PARTS : 5 * PARTS], refs[5 * PARTS :]
    half = KV_WIDTH // PARTS
    for part in range(PARTS):
        assemble(fa, own[2 * part], own[2 * part + 1], place, count, rows, part * half)
        assemble(fb, late[2 * part], late[2 * part + 1], place, count, rows, part * half)
    even = place[2] == 0
    gk = jnp.concatenate([g[:, :half] for g in grads], axis=1)
    gv = jnp.concatenate([g[:, half:] for g in grads], axis=1)
    ga = jnp.where(even, gk, gv)
    gb = jnp.where(even, gv, gk)
    out[...] = (nt(ga, fa[...]) + nt(gb, fb[...])).astype(jnp.bfloat16)


def input_grad_of(place, grads, own, late, count, rows):
    full = pltpu.VMEM((2 * count * rows, KV_WIDTH), jnp.bfloat16)
    operands = [*grads, *own, *late]
    return pl.pallas_call(
        functools.partial(input_grad_kernel, count=count, rows=rows),
        in_specs=[sspec()] + [vspec()] * len(operands),
        out_specs=vspec(),
        out_shape=jax.ShapeDtypeStruct((grads[0].shape[0], 2 * count * rows), jnp.bfloat16),
        scratch_shapes=[full, full],
        compiler_params=params(),
        name="input_grad",
    )(place, *near(*operands))


def turn_kernel(place, here, *refs, count, rows):
    wrapped, returned, out = refs[: count - 1], refs[count - 1 : 2 * count - 2], refs[-1]
    block = here.shape[0]
    for k in range(count):
        if k == 0:
            got = here[...]
        else:
            got = jnp.where(place[0] >= k, returned[count - k - 1][...], wrapped[k - 1][:block, :])
        for core in range(2):
            at = (2 * k + core) * block
            out[:, at : at + block] = got[:, core * rows : (core + 1) * rows].T


def turn(place, here, wrapped, returned, rows):
    count = len(wrapped) + 1
    return pl.pallas_call(
        functools.partial(turn_kernel, count=count, rows=rows),
        in_specs=[sspec()] + [vspec()] * (2 * count - 1),
        out_specs=vspec(),
        out_shape=pltpu.VMEM((rows, 2 * count * here.shape[0]), here.dtype),
        compiler_params=params(),
        name="turn",
    )(place, *near(here, *wrapped, *returned))


def weight_grad_kernel(x_turned, g_own, g_other, out, *, count):
    size = g_own.shape[0] // count
    pieces = []
    for k in range(count):
        pieces += [g_own[k * size : (k + 1) * size, :], g_other[k * size : (k + 1) * size, :]]
    grads = jnp.concatenate(pieces, axis=0)
    out[...] = jnp.dot(x_turned[...], grads, preferred_element_type=jnp.float32).astype(jnp.bfloat16)


def weight_grad_of(x_turned, g_own, g_other, count):
    return pl.pallas_call(
        functools.partial(weight_grad_kernel, count=count),
        in_specs=[vspec()] * 3,
        out_specs=vspec(),
        out_shape=pltpu.VMEM((x_turned.shape[0], g_own.shape[1]), jnp.bfloat16),
        compiler_params=params(),
        name="weight_grad",
    )(*near(x_turned, g_own, g_other))


def finish_kernel(place, *refs):
    pairs, outs = refs[:-2], refs[-2:]
    half = KV_WIDTH // PARTS
    for part in range(PARTS):
        a, b = pairs[2 * part], pairs[2 * part + 1]
        grad = (a[...].astype(jnp.float32) + b[...].astype(jnp.float32)).astype(jnp.bfloat16)
        left = pl.multiple_of((place[3] if part == 0 else 1 - place[3]) * half, half)
        outs[0][:, pl.ds(left, half)] = grad[:, :half]
        outs[1][:, pl.ds(left, half)] = grad[:, half:]


def finish(place, *partials):
    out = jax.ShapeDtypeStruct((partials[0].shape[0], KV_WIDTH), jnp.bfloat16)
    return pl.pallas_call(
        finish_kernel,
        in_specs=[sspec()] + [vspec()] * len(partials),
        out_specs=[vspec()] * 2,
        out_shape=[out, out],
        compiler_params=params(),
        name="finish",
    )(place, *near(*partials))


def body(activations, queries, key_weight, value_weight, segment_ids, out_grad):
    inputs = activations[0]
    block = inputs.shape[0]
    rows = key_weight.shape[0]
    n = lax.axis_size("seq")
    reps = lax.axis_size("rep")
    z, c = lax.axis_index("seq"), lax.axis_index("fsdp")
    odd = lax.rem(lax.axis_index("rep"), 2)
    turned = lax.rem(lax.axis_index("groups"), 2)
    place = jnp.stack([z, c, odd, turned]).astype(jnp.int32)
    shifts = range(1, n)
    cut_at = KV_WIDTH // PARTS

    def around(x, k):
        return lax.ppermute(x, "seq", [(i, (i + k) % n) for i in range(n)])

    def up(x, k):
        return lax.ppermute(x, "seq", [(i, i + k) for i in range(n - k)])

    def down(x, k):
        return lax.ppermute(x, "seq", [(i, i - k) for i in range(k, n)])

    def pairwise(x, axis):
        return lax.ppermute(x, axis, [(j, j ^ 1) for j in range(lax.axis_size(axis))])

    def partner(x):
        return pairwise(x, "rep")

    def core(x):
        return pairwise(x, "fsdp")

    half = jnp.where(odd == 0, key_weight, value_weight)
    half = lax.dynamic_slice_in_dim(half, turned * cut_at, cut_at, 1)
    gathered = [half] + [around(half, k) for k in shifts]
    x_next = partner(inputs)
    x_for = cut(place, inputs, core(inputs), n, rows)
    gathered, x_next, x_for = lax.optimization_barrier((gathered, x_next, x_for))
    w_own = [jnp.concatenate(gathered, axis=0)]
    w_other = [core(w_own[0])]
    w_across = pairwise(w_own[0], "groups")

    own, other = project(place, segment_ids, inputs, x_next, w_own[0], w_other[0], n, rows)
    pair, loads = pack(place, own, partner(other), x_for[1:])
    carried = [around(x, k) for k, x in zip(shifts, loads)]
    w_across, _ = lax.optimization_barrier((w_across, loads[0]))
    w_own.append(w_across)
    w_other.append(core(w_across))
    own_2, other_2 = project(place, segment_ids, inputs, x_next, w_own[1], w_other[1], n, rows)
    mate_2, _ = lax.optimization_barrier((partner(other_2), carried))
    pair_2 = jnp.concatenate([own_2[:block], mate_2], axis=1)
    ups = [up(pair_2, k) for k in shifts]

    w_late, _ = lax.optimization_barrier((w_own, carried[0]))
    b_own = [partner(w) for w in w_late]
    queries, out_grad = queries[0], out_grad[0]
    before, sent_a, own_a = attend(
        place, queries, out_grad, [pair] + carried, 0, x_for[:0:-1], []
    )
    returned = [around(x, n - k) for k, x in zip(shifts, sent_a)]
    before, sent_b, own_b = attend(place, queries, out_grad, [pair_2] + ups, 1, [], before)
    back_b = [down(x, k) for k, x in zip(shifts, sent_b)]
    back_b, b_own = lax.optimization_barrier((back_b, b_own))
    b_other = [core(b) for b in b_own]
    returned, _ = lax.optimization_barrier((returned, sent_b))
    back_a = [jnp.where(z + k < n, x, jnp.zeros_like(x)) for k, x in zip(shifts, returned)]
    sums = []
    for total, back in ((own_a, back_a), (own_b, back_b)):
        for x in back:
            total = total + x.astype(jnp.float32)
        sums.append(total.astype(jnp.bfloat16))
    context, query_grad = before[:2]
    x_turned = turn(place, x_for[0], carried, returned, rows)

    partials = []
    for part in range(PARTS):
        pieces = [sums[part]] + [around(sums[part], k) for k in shifts]
        if part == 0:
            pieces, _ = lax.optimization_barrier((pieces, sums[1]))
        else:
            pieces, partials = lax.optimization_barrier((pieces, partials))
        g_own = jnp.concatenate(pieces, axis=0)
        partials.append(weight_grad_of(x_turned, g_own, core(g_own), n))
    sums, _ = lax.optimization_barrier((sums, partials[-1]))
    own_weights = [w_own[0], w_other[0], w_own[1], w_other[1]]
    input_grad = input_grad_of(place, sums, own_weights, [b_own[0], b_other[0], b_own[1], b_other[1]], n, rows)
    if reps == 2:
        others = [partner(p) for p in partials]
        others, input_grad = lax.optimization_barrier((others, input_grad))
        grads = finish(place, *[x for p in zip(partials, others) for x in p])
    else:
        totals = [lax.psum(p.astype(jnp.float32), "rep").astype(jnp.bfloat16) for p in partials]
        grads = finish(place, *[x for p in totals for x in (p, jnp.zeros_like(p))])
    return context[None], query_grad[None], input_grad[None], grads[0], grads[1]


def solution(mesh):
    return jax.shard_map(
        body,
        mesh=mesh,
        in_specs=(
            P(("groups", "rep", "fsdp"), "seq", None),
            P(("groups", "rep", "fsdp"), "seq", None),
            P(("seq", "fsdp"), None),
            P(("seq", "fsdp"), None),
            P(("groups", "rep", "fsdp"), "seq"),
            P(("groups", "rep", "fsdp"), "seq", None),
        ),
        out_specs=(
            P(("groups", "rep", "fsdp"), "seq", None),
            P(("groups", "rep", "fsdp"), "seq", None),
            P(("groups", "rep", "fsdp"), "seq", None),
            P(("groups", "seq", "fsdp"), None),
            P(("groups", "seq", "fsdp"), None),
        ),
        check_vma=False,
    )
```

```python
import functools
import math

import jax
import jax.numpy as jnp
from jax import lax
from jax.experimental import pallas as pl
from jax.experimental.pallas import tpu as pltpu
from jax.sharding import PartitionSpec as P

HEADS = 16
KV_HEADS = 4
HEAD_DIM = 128
KV_WIDTH = KV_HEADS * HEAD_DIM
GROUP = HEADS // KV_HEADS
PARTS = 2
LOG2E = 1.4426950408889634
MASKED = -1e30
EXTRA = 16
LIGHT = pl.CostEstimate(flops=0, transcendentals=0, bytes_accessed=0)
MIB = 1024 * 1024


def far(*xs):
    return [pltpu.with_memory_space_constraint(x, pltpu.HBM) for x in xs]


def params(mib=16, **kw):
    return pltpu.CompilerParams(vmem_limit_bytes=mib * MIB, **kw)


def vspec():
    return pl.BlockSpec(memory_space=pltpu.VMEM)


def near(*xs):
    return [pltpu.with_memory_space_constraint(x, pltpu.VMEM) for x in xs]


def sspec():
    return pl.BlockSpec(memory_space=pltpu.SMEM)


def assemble(full_ref, own_ref, other_ref, place, count, rows, left=0):
    z, c = place[0], place[1]
    right = left + own_ref.shape[1]
    for k in range(count):
        src = lax.rem(z - k + count, count)
        for ref, core in ((own_ref, c), (other_ref, 1 - c)):
            start = pl.multiple_of((src * 2 + core) * rows, rows)
            full_ref[pl.ds(start, rows), left:right] = ref[k * rows : (k + 1) * rows, :]


def project_kernel(place, seg, x_own, x_next, w_own, w_other, out_own, out_next, full, *, count, rows):
    assemble(full, w_own, w_other, place, count, rows)
    w = full[...]
    block = x_own.shape[0]
    out_next[...] = jnp.dot(x_next[...], w, preferred_element_type=jnp.float32).astype(jnp.bfloat16)
    out_own[:block, :] = jnp.dot(x_own[...], w, preferred_element_type=jnp.float32).astype(
        jnp.bfloat16
    )
    ids = (seg[...] + 1).astype(jnp.float32)
    copies = out_own.shape[1] // block
    wide = jnp.concatenate([jnp.broadcast_to(ids, (EXTRA, block))] * copies, axis=1)
    out_own[block:, :] = wide.astype(jnp.bfloat16)


def project(place, seg, x_own, x_next, w_own, w_other, count, rows):
    width = w_own.shape[1]
    block = x_own.shape[0]
    return pl.pallas_call(
        functools.partial(project_kernel, count=count, rows=rows),
        in_specs=[sspec()] + [vspec()] * 5,
        out_specs=[vspec()] * 2,
        out_shape=[
            pltpu.VMEM((block + EXTRA, width), jnp.bfloat16),
            pltpu.VMEM((block, width), jnp.bfloat16),
        ],
        scratch_shapes=[pltpu.VMEM((2 * count * rows, width), jnp.bfloat16)],
        compiler_params=params(),
        name="project",
    )(place, seg, x_own, *near(x_next, w_own, w_other))


def cut_kernel(place, own, other, *outs, count, rows):
    for k in range(count):
        start = (lax.rem(place[0] + k, count) * 2 + place[1]) * rows
        start = pl.multiple_of(start, rows)
        outs[k][:, :rows] = own[:, pl.ds(start, rows)]
        outs[k][:, rows:] = other[:, pl.ds(start, rows)]


def cut(place, own, other, count, rows):
    block = own.shape[0]
    if rows % 128 or 2 * rows != KV_WIDTH:
        pieces = []
        for k in range(count):
            start = (lax.rem(place[0] + k, count) * 2 + place[1]) * rows
            both = [lax.dynamic_slice_in_dim(x, start, rows, 1) for x in (own, other)]
            wide = jnp.concatenate(both, axis=1)
            pieces.append(jnp.pad(wide, ((0, 0), (0, KV_WIDTH - 2 * rows))))
        return pieces
    return pl.pallas_call(
        functools.partial(cut_kernel, count=count, rows=rows),
        in_specs=[sspec()] + [vspec()] * 2,
        out_specs=[vspec()] * count,
        out_shape=[pltpu.VMEM((block, 2 * rows), own.dtype)] * count,
        compiler_params=params(),
        name="cut",
    )(place, own, *near(other))


def pack_kernel(place, own, mate, *refs, count):
    cols, outs = refs[: count - 1], refs[count - 1 :]
    block, half = mate.shape
    first = jnp.concatenate([own[:block, :], mate[...]], axis=1)
    tail = own[block:, :]
    outs[0][:block, :] = first
    outs[0][block:, :half] = tail
    outs[0][block:, half:] = jnp.zeros_like(tail)
    for k in range(1, count):
        goes_up = place[0] + k < count
        outs[k][:block, :] = jnp.where(goes_up, first, cols[k - 1][...])
        outs[k][block:, :half] = jnp.where(goes_up, tail, jnp.zeros_like(tail))
        outs[k][block:, half:] = jnp.zeros_like(tail)


def pack(place, own, mate, cols):
    count = len(cols) + 1
    tall = pltpu.VMEM((own.shape[0], 2 * own.shape[1]), own.dtype)
    outs = pl.pallas_call(
        functools.partial(pack_kernel, count=count),
        in_specs=[sspec()] + [vspec()] * (count + 1),
        out_specs=[vspec()] * count,
        out_shape=[tall] * count,
        compiler_params=params(),
        name="pack",
    )(place, *near(own, mate, *cols))
    return outs[0], outs[1:]


def nt(a, b):
    return lax.dot_general(a, b, (((1,), (1,)), ((), ())), preferred_element_type=jnp.float32)


def tn(a, b):
    return lax.dot_general(a, b, (((0,), (0,)), ((), ())), preferred_element_type=jnp.float32)


def attend_kernel(place, q_ref, do_ref, *refs, count, block, opening):
    pair_refs, refs = refs[:count], refs[count:]
    if opening:
        cols = refs[: count - 1]
        ctx_ref, dq_ref, bias = refs[count - 1 : count + 2]
        grads, own_grad = refs[count + 2 : -1], refs[-1]
    else:
        bias = refs[0]
        ctx_ref, dq_ref = refs[3:5]
        grads, own_grad = refs[5:-1], refs[-1]
    inv_root = 1.0 / math.sqrt(HEAD_DIM)
    length = count * block

    if opening:

        @pl.when(pl.program_id(0) == 0)
        def _():
            ids = [r[block : block + 1, :block].astype(jnp.float32) for r in pair_refs]
            mine = jnp.broadcast_to(ids[0], (block, block)).T
            rows = lax.broadcasted_iota(jnp.int32, (block, block), 0)
            cols_here = lax.broadcasted_iota(jnp.int32, (block, block), 1)
            for k in range(count):
                ok = mine == jnp.broadcast_to(ids[k], (block, block))
                if k == 0:
                    ok = ok & (cols_here <= rows)
                bias[:, k * block : (k + 1) * block] = jnp.where(ok, 0.0, MASKED)

    even = place[2] == 0
    at_key = pl.multiple_of(pl.program_id(0) * HEAD_DIM, HEAD_DIM)
    at_value = pl.multiple_of(at_key + KV_WIDTH // PARTS, HEAD_DIM)
    a = jnp.concatenate([r[:block, pl.ds(at_key, HEAD_DIM)] for r in pair_refs], axis=0)
    b = jnp.concatenate([r[:block, pl.ds(at_value, HEAD_DIM)] for r in pair_refs], axis=0)
    key = jnp.where(even, a, b)
    value = jnp.where(even, b, a)

    def stack(ref):
        return jnp.concatenate(
            [ref[:, h * HEAD_DIM : (h + 1) * HEAD_DIM] for h in range(GROUP)], axis=0
        )

    def unstack(ref, val):
        for h in range(GROUP):
            ref[:, h * HEAD_DIM : (h + 1) * HEAD_DIM] = val[h * block : (h + 1) * block, :]

    q, do = stack(q_ref), stack(do_ref)
    s = nt(q, key) * (inv_root * LOG2E)
    s = (s.reshape(GROUP, block, length) + bias[...][None]).reshape(GROUP * block, length)
    e = jnp.exp2(s - jnp.max(s, axis=1, keepdims=True))
    p = e * (1.0 / jnp.sum(e, axis=1, keepdims=True))
    p_low = p.astype(jnp.bfloat16)
    ctx = jnp.dot(p_low, value, preferred_element_type=jnp.float32).astype(jnp.bfloat16)
    unstack(ctx_ref, ctx)
    dots = jnp.sum(do.astype(jnp.float32) * ctx.astype(jnp.float32), axis=1, keepdims=True)
    ds = (p * (nt(do, value) - dots)).astype(jnp.bfloat16)
    dq = jnp.dot(ds, key, preferred_element_type=jnp.float32) * inv_root
    unstack(dq_ref, dq.astype(jnp.bfloat16))
    dv = tn(do, p_low).T
    dk = (tn(q, ds) * inv_root).T
    own_grad[:, pl.ds(at_key, HEAD_DIM)] = dk[:block]
    own_grad[:, pl.ds(at_value, HEAD_DIM)] = dv[:block]
    for k in range(1, count):
        piece = slice(k * block, (k + 1) * block)
        for at, grad in ((at_key, dk), (at_value, dv)):
            sent = grad[piece].astype(jnp.bfloat16)
            if opening:
                sent = jnp.where(place[0] >= k, sent, cols[k - 1][:, pl.ds(at, HEAD_DIM)])
            grads[k - 1][:, pl.ds(at, HEAD_DIM)] = sent


def attend(place, q, do, pairs, part, cols, before):
    block, width = q.shape
    count = len(pairs)
    steps = KV_HEADS // PARTS
    opening = not before

    def at_part(g, place):
        return (0, (place[3] if part == 0 else 1 - place[3]) * steps + g)

    wide = pl.BlockSpec((block, GROUP * HEAD_DIM), at_part)
    both = 2 * KV_WIDTH // PARTS
    rows = jax.ShapeDtypeStruct((block, width), jnp.bfloat16)
    own = pltpu.HBM((block, both), jnp.float32)
    sent = pltpu.VMEM((block, both), jnp.bfloat16)
    operands = [place, q, do, *(near(*pairs) if opening else far(*pairs))]
    in_specs = [wide, wide] + [vspec()] * count
    if opening:
        operands += near(*cols)
        in_specs += [vspec()] * (count - 1)
        out_specs = [wide, wide, vspec()] + [vspec()] * count
        out_shape = [rows, rows, pltpu.HBM((block, count * block), jnp.float32)]
        aliases = {}
    else:
        context, query_grad, mask = before
        aliases = {len(operands) + 1: 0, len(operands) + 2: 1}
        operands += [*far(mask), context, query_grad]
        in_specs += [vspec()] + [pl.BlockSpec(memory_space=pl.ANY)] * 2
        out_specs = [wide, wide] + [vspec()] * count
        out_shape = [rows, rows]
    outs = pl.pallas_call(
        functools.partial(attend_kernel, count=count, block=block, opening=opening),
        grid_spec=pltpu.PrefetchScalarGridSpec(
            num_scalar_prefetch=1, grid=(steps,), in_specs=in_specs, out_specs=out_specs
        ),
        out_shape=out_shape + [sent] * (count - 1) + [own],
        input_output_aliases=aliases,
        compiler_params=params(4 + 3 * count, dimension_semantics=("arbitrary",)),
        name="attend",
    )(*operands)
    return outs[: len(outs) - count], outs[len(outs) - count : -1], outs[-1]


def input_grad_kernel(place, *refs, count, rows):
    grads = refs[:PARTS]
    own = refs[PARTS : 3 * PARTS]
    b_own, b_other, out, fa, fb = refs[3 * PARTS :]
    half = KV_WIDTH // PARTS
    for part in range(PARTS):
        assemble(fa, own[2 * part], own[2 * part + 1], place, count, rows, part * half)
    assemble(fb, b_own, b_other, place, count, rows)
    even = place[2] == 0
    gk = jnp.concatenate([g[:, :half] for g in grads], axis=1)
    gv = jnp.concatenate([g[:, half:] for g in grads], axis=1)
    ga = jnp.where(even, gk, gv)
    gb = jnp.where(even, gv, gk)
    out[...] = (nt(ga, fa[...]) + nt(gb, fb[...])).astype(jnp.bfloat16)


def input_grad_of(place, grads, own, b_own, b_other, count, rows):
    full = pltpu.VMEM((2 * count * rows, KV_WIDTH), jnp.bfloat16)
    operands = [*grads, *own, b_own, b_other]
    return pl.pallas_call(
        functools.partial(input_grad_kernel, count=count, rows=rows),
        in_specs=[sspec()] + [vspec()] * len(operands),
        out_specs=vspec(),
        out_shape=jax.ShapeDtypeStruct((grads[0].shape[0], 2 * count * rows), jnp.bfloat16),
        scratch_shapes=[full, full],
        compiler_params=params(),
        name="input_grad",
    )(place, *near(*operands))


def turn_kernel(place, here, *refs, count, rows):
    wrapped, returned, out = refs[: count - 1], refs[count - 1 : 2 * count - 2], refs[-1]
    block = here.shape[0]
    for k in range(count):
        if k == 0:
            got = here[...]
        else:
            got = jnp.where(place[0] >= k, returned[count - k - 1][...], wrapped[k - 1][:block, :])
        for core in range(2):
            at = (2 * k + core) * block
            out[:, at : at + block] = got[:, core * rows : (core + 1) * rows].T


def turn(place, here, wrapped, returned, rows):
    count = len(wrapped) + 1
    return pl.pallas_call(
        functools.partial(turn_kernel, count=count, rows=rows),
        in_specs=[sspec()] + [vspec()] * (2 * count - 1),
        out_specs=vspec(),
        out_shape=pltpu.VMEM((rows, 2 * count * here.shape[0]), here.dtype),
        compiler_params=params(),
        name="turn",
    )(place, *near(here, *wrapped, *returned))


def weight_grad_kernel(x_turned, g_own, g_other, out, *, count):
    size = g_own.shape[0] // count
    pieces = []
    for k in range(count):
        pieces += [g_own[k * size : (k + 1) * size, :], g_other[k * size : (k + 1) * size, :]]
    grads = jnp.concatenate(pieces, axis=0)
    out[...] = jnp.dot(x_turned[...], grads, preferred_element_type=jnp.float32).astype(jnp.bfloat16)


def weight_grad_of(x_turned, g_own, g_other, count):
    return pl.pallas_call(
        functools.partial(weight_grad_kernel, count=count),
        in_specs=[vspec()] * 3,
        out_specs=vspec(),
        out_shape=pltpu.VMEM((x_turned.shape[0], g_own.shape[1]), jnp.bfloat16),
        compiler_params=params(),
        name="weight_grad",
    )(*near(x_turned, g_own, g_other))


def finish_kernel(place, *refs):
    pairs, outs = refs[:-2], refs[-2:]
    half = KV_WIDTH // PARTS
    for part in range(PARTS):
        a, b = pairs[2 * part], pairs[2 * part + 1]
        grad = (a[...].astype(jnp.float32) + b[...].astype(jnp.float32)).astype(jnp.bfloat16)
        left = pl.multiple_of((place[3] if part == 0 else 1 - place[3]) * half, half)
        outs[0][:, pl.ds(left, half)] = grad[:, :half]
        outs[1][:, pl.ds(left, half)] = grad[:, half:]


def finish(place, *partials):
    out = jax.ShapeDtypeStruct((partials[0].shape[0], KV_WIDTH), jnp.bfloat16)
    return pl.pallas_call(
        finish_kernel,
        in_specs=[sspec()] + [vspec()] * len(partials),
        out_specs=[vspec()] * 2,
        out_shape=[out, out],
        compiler_params=params(),
        name="finish",
    )(place, *near(*partials))


def body(activations, queries, key_weight, value_weight, segment_ids, out_grad):
    inputs = activations[0]
    block = inputs.shape[0]
    rows = key_weight.shape[0]
    n = lax.axis_size("seq")
    reps = lax.axis_size("rep")
    z, c = lax.axis_index("seq"), lax.axis_index("fsdp")
    odd = lax.rem(lax.axis_index("rep"), 2)
    turned = lax.rem(lax.axis_index("groups"), 2)
    place = jnp.stack([z, c, odd, turned]).astype(jnp.int32)
    shifts = range(1, n)
    cut_at = KV_WIDTH // PARTS

    def around(x, k):
        return lax.ppermute(x, "seq", [(i, (i + k) % n) for i in range(n)])

    def up(x, k):
        return lax.ppermute(x, "seq", [(i, i + k) for i in range(n - k)])

    def down(x, k):
        return lax.ppermute(x, "seq", [(i, i - k) for i in range(k, n)])

    def pairwise(x, axis):
        return lax.ppermute(x, axis, [(j, j ^ 1) for j in range(lax.axis_size(axis))])

    def partner(x):
        return pairwise(x, "rep")

    def core(x):
        return pairwise(x, "fsdp")

    half = jnp.where(odd == 0, key_weight, value_weight)
    half = lax.dynamic_slice_in_dim(half, turned * cut_at, cut_at, 1)
    gathered = [half] + [around(half, k) for k in shifts]
    x_next = partner(inputs)
    x_for = cut(place, inputs, core(inputs), n, rows)
    gathered, x_next, x_for = lax.optimization_barrier((gathered, x_next, x_for))
    w_own = [jnp.concatenate(gathered, axis=0)]
    w_other = [core(w_own[0])]
    w_across = pairwise(w_own[0], "groups")

    own, other = project(place, segment_ids, inputs, x_next, w_own[0], w_other[0], n, rows)
    pair, loads = pack(place, own, partner(other), x_for[1:])
    carried = [around(x, k) for k, x in zip(shifts, loads)]
    w_across, _ = lax.optimization_barrier((w_across, loads[0]))
    w_own.append(w_across)
    w_other.append(core(w_across))
    own_2, other_2 = project(place, segment_ids, inputs, x_next, w_own[1], w_other[1], n, rows)
    mate_2, _ = lax.optimization_barrier((partner(other_2), carried))
    pair_2 = jnp.concatenate([own_2[:block], mate_2], axis=1)
    ups = [up(pair_2, k) for k in shifts]

    w_late, _ = lax.optimization_barrier((w_own, pair_2))
    b_own = partner(jnp.concatenate(w_late, axis=1))
    carried, _ = lax.optimization_barrier((carried, pair_2))
    queries, out_grad = queries[0], out_grad[0]
    before, sent_a, own_a = attend(
        place, queries, out_grad, [pair] + carried, 0, x_for[:0:-1], []
    )
    returned = [around(x, n - k) for k, x in zip(shifts, sent_a)]
    before, sent_b, own_b = attend(place, queries, out_grad, [pair_2] + ups, 1, [], before)
    sent_b, returned, b_own = lax.optimization_barrier((sent_b, returned, b_own))
    back_b = [down(x, k) for k, x in zip(shifts, sent_b)]
    b_other = core(b_own)
    back_a = [jnp.where(z + k < n, x, jnp.zeros_like(x)) for k, x in zip(shifts, returned)]
    sums = []
    for total, back in ((own_a, back_a), (own_b, back_b)):
        for x in back:
            total = total + x.astype(jnp.float32)
        sums.append(total.astype(jnp.bfloat16))
    context, query_grad = before[:2]
    x_turned = turn(place, x_for[0], carried, returned, rows)

    partials = []
    for part in range(PARTS):
        pieces = [sums[part]] + [around(sums[part], k) for k in shifts]
        if part == 0:
            pieces, _ = lax.optimization_barrier((pieces, sums[1]))
        else:
            pieces, partials = lax.optimization_barrier((pieces, partials))
        g_own = jnp.concatenate(pieces, axis=0)
        partials.append(weight_grad_of(x_turned, g_own, core(g_own), n))
    sums, _ = lax.optimization_barrier((sums, partials[-1]))
    own_weights = [w_own[0], w_other[0], w_own[1], w_other[1]]
    input_grad = input_grad_of(place, sums, own_weights, b_own, b_other, n, rows)
    if reps == 2:
        others = [partner(p) for p in partials]
        others, input_grad = lax.optimization_barrier((others, input_grad))
        grads = finish(place, *[x for p in zip(partials, others) for x in p])
    else:
        totals = [lax.psum(p.astype(jnp.float32), "rep").astype(jnp.bfloat16) for p in partials]
        grads = finish(place, *[x for p in totals for x in (p, jnp.zeros_like(p))])
    return context[None], query_grad[None], input_grad[None], grads[0], grads[1]


def solution(mesh):
    return jax.shard_map(
        body,
        mesh=mesh,
        in_specs=(
            P(("groups", "rep", "fsdp"), "seq", None),
            P(("groups", "rep", "fsdp"), "seq", None),
            P(("seq", "fsdp"), None),
            P(("seq", "fsdp"), None),
            P(("groups", "rep", "fsdp"), "seq"),
            P(("groups", "rep", "fsdp"), "seq", None),
        ),
        out_specs=(
            P(("groups", "rep", "fsdp"), "seq", None),
            P(("groups", "rep", "fsdp"), "seq", None),
            P(("groups", "rep", "fsdp"), "seq", None),
            P(("groups", "seq", "fsdp"), None),
            P(("groups", "seq", "fsdp"), None),
        ),
        check_vma=False,
    )
```

```python
import functools
import math

import jax
import jax.numpy as jnp
from jax import lax
from jax.experimental import pallas as pl
from jax.experimental.pallas import tpu as pltpu
from jax.sharding import PartitionSpec as P

HEADS = 16
KV_HEADS = 4
HEAD_DIM = 128
KV_WIDTH = KV_HEADS * HEAD_DIM
GROUP = HEADS // KV_HEADS
PARTS = 2
LOG2E = 1.4426950408889634
MASKED = -1e30
EXTRA = 16
LIGHT = pl.CostEstimate(flops=0, transcendentals=0, bytes_accessed=0)
MIB = 1024 * 1024


def far(*xs):
    return [pltpu.with_memory_space_constraint(x, pltpu.HBM) for x in xs]


def params(mib=16, **kw):
    return pltpu.CompilerParams(vmem_limit_bytes=mib * MIB, **kw)


def vspec():
    return pl.BlockSpec(memory_space=pltpu.VMEM)


def near(*xs):
    return [pltpu.with_memory_space_constraint(x, pltpu.VMEM) for x in xs]


def sspec():
    return pl.BlockSpec(memory_space=pltpu.SMEM)


def assemble(full_ref, own_ref, other_ref, place, count, rows):
    z, c = place[0], place[1]
    for k in range(count):
        src = lax.rem(z - k + count, count)
        for ref, core in ((own_ref, c), (other_ref, 1 - c)):
            start = pl.multiple_of((src * 2 + core) * rows, rows)
            full_ref[pl.ds(start, rows), :] = ref[k * rows : (k + 1) * rows, :]


def project_kernel(place, seg, x_own, x_next, w_own, w_other, out_own, out_next, full, *, count, rows):
    assemble(full, w_own, w_other, place, count, rows)
    w = full[...]
    block = x_own.shape[0]
    out_next[...] = jnp.dot(x_next[...], w, preferred_element_type=jnp.float32).astype(jnp.bfloat16)
    out_own[:block, :] = jnp.dot(x_own[...], w, preferred_element_type=jnp.float32).astype(
        jnp.bfloat16
    )
    ids = (seg[...] + 1).astype(jnp.float32)
    copies = out_own.shape[1] // block
    wide = jnp.concatenate([jnp.broadcast_to(ids, (EXTRA, block))] * copies, axis=1)
    out_own[block:, :] = wide.astype(jnp.bfloat16)


def project(place, seg, x_own, x_next, w_own, w_other, count, rows):
    width = w_own.shape[1]
    block = x_own.shape[0]
    return pl.pallas_call(
        functools.partial(project_kernel, count=count, rows=rows),
        in_specs=[sspec()] + [vspec()] * 5,
        out_specs=[vspec()] * 2,
        out_shape=[
            pltpu.VMEM((block + EXTRA, width), jnp.bfloat16),
            pltpu.VMEM((block, width), jnp.bfloat16),
        ],
        scratch_shapes=[pltpu.VMEM((2 * count * rows, width), jnp.bfloat16)],
        compiler_params=params(),
        name="project",
    )(place, seg, x_own, x_next, *near(w_own, w_other))


def cut_kernel(place, own, other, *outs, count, rows):
    for k in range(count):
        start = (lax.rem(place[0] + k, count) * 2 + place[1]) * rows
        start = pl.multiple_of(start, rows)
        outs[k][:, :rows] = own[:, pl.ds(start, rows)]
        outs[k][:, rows:] = other[:, pl.ds(start, rows)]


def cut(place, own, other, count, rows):
    block = own.shape[0]
    if rows % 128 or 2 * rows != KV_WIDTH:
        pieces = []
        for k in range(count):
            start = (lax.rem(place[0] + k, count) * 2 + place[1]) * rows
            both = [lax.dynamic_slice_in_dim(x, start, rows, 1) for x in (own, other)]
            wide = jnp.concatenate(both, axis=1)
            pieces.append(jnp.pad(wide, ((0, 0), (0, KV_WIDTH - 2 * rows))))
        return pieces
    return pl.pallas_call(
        functools.partial(cut_kernel, count=count, rows=rows),
        in_specs=[sspec()] + [vspec()] * 2,
        out_specs=[vspec()] * count,
        out_shape=[pltpu.VMEM((block, 2 * rows), own.dtype)] * count,
        compiler_params=params(),
        name="cut",
    )(place, own, *near(other))


def pack_kernel(place, own, mate, *refs, count):
    cols, outs = refs[: count - 1], refs[count - 1 :]
    block, width = mate.shape
    half = width // PARTS
    first = jnp.concatenate([own[:block, :half], mate[:, :half]], axis=1)
    tail = own[block:, :]
    outs[0][:block, :] = first
    outs[0][block:, :] = tail
    outs[1][...] = jnp.concatenate([own[:block, half:], mate[:, half:]], axis=1)
    for k in range(1, count):
        goes_up = place[0] + k < count
        outs[k + 1][:block, :] = jnp.where(goes_up, first, cols[k - 1][...])
        outs[k + 1][block:, :] = jnp.where(goes_up, tail, jnp.zeros_like(tail))


def pack(place, own, mate, cols):
    count = len(cols) + 1
    tall = pltpu.VMEM(own.shape, own.dtype)
    outs = pl.pallas_call(
        functools.partial(pack_kernel, count=count),
        in_specs=[sspec()] + [vspec()] * (count + 1),
        out_specs=[vspec()] * (count + 1),
        out_shape=[tall, pltpu.VMEM(mate.shape, mate.dtype)] + [tall] * (count - 1),
        compiler_params=params(),
        name="pack",
    )(place, *near(own, mate, *cols))
    return outs[0], outs[1], outs[2:]


def nt(a, b):
    return lax.dot_general(a, b, (((1,), (1,)), ((), ())), preferred_element_type=jnp.float32)


def tn(a, b):
    return lax.dot_general(a, b, (((0,), (0,)), ((), ())), preferred_element_type=jnp.float32)


def attend_kernel(place, q_ref, do_ref, *refs, count, block, opening):
    pair_refs, refs = refs[:count], refs[count:]
    if opening:
        cols = refs[: count - 1]
        ctx_ref, dq_ref, bias = refs[count - 1 : count + 2]
        grads, own_grad = refs[count + 2 : -1], refs[-1]
    else:
        bias = refs[0]
        ctx_ref, dq_ref = refs[3:5]
        grads, own_grad = refs[5:-1], refs[-1]
    inv_root = 1.0 / math.sqrt(HEAD_DIM)
    length = count * block

    if opening:

        @pl.when(pl.program_id(0) == 0)
        def _():
            ids = [r[block : block + 1, :block].astype(jnp.float32) for r in pair_refs]
            mine = jnp.broadcast_to(ids[0], (block, block)).T
            rows = lax.broadcasted_iota(jnp.int32, (block, block), 0)
            cols_here = lax.broadcasted_iota(jnp.int32, (block, block), 1)
            for k in range(count):
                ok = mine == jnp.broadcast_to(ids[k], (block, block))
                if k == 0:
                    ok = ok & (cols_here <= rows)
                bias[:, k * block : (k + 1) * block] = jnp.where(ok, 0.0, MASKED)

    even = place[2] == 0
    at_key = pl.multiple_of(pl.program_id(0) * HEAD_DIM, HEAD_DIM)
    at_value = pl.multiple_of(at_key + KV_WIDTH // PARTS, HEAD_DIM)
    a = jnp.concatenate([r[:block, pl.ds(at_key, HEAD_DIM)] for r in pair_refs], axis=0)
    b = jnp.concatenate([r[:block, pl.ds(at_value, HEAD_DIM)] for r in pair_refs], axis=0)
    key = jnp.where(even, a, b)
    value = jnp.where(even, b, a)

    def stack(ref):
        return jnp.concatenate(
            [ref[:, h * HEAD_DIM : (h + 1) * HEAD_DIM] for h in range(GROUP)], axis=0
        )

    def unstack(ref, val):
        for h in range(GROUP):
            ref[:, h * HEAD_DIM : (h + 1) * HEAD_DIM] = val[h * block : (h + 1) * block, :]

    q, do = stack(q_ref), stack(do_ref)
    s = nt(q, key) * (inv_root * LOG2E)
    s = (s.reshape(GROUP, block, length) + bias[...][None]).reshape(GROUP * block, length)
    e = jnp.exp2(s - jnp.max(s, axis=1, keepdims=True))
    p = e * (1.0 / jnp.sum(e, axis=1, keepdims=True))
    p_low = p.astype(jnp.bfloat16)
    ctx = jnp.dot(p_low, value, preferred_element_type=jnp.float32).astype(jnp.bfloat16)
    unstack(ctx_ref, ctx)
    dots = jnp.sum(do.astype(jnp.float32) * ctx.astype(jnp.float32), axis=1, keepdims=True)
    ds = (p * (nt(do, value) - dots)).astype(jnp.bfloat16)
    dq = jnp.dot(ds, key, preferred_element_type=jnp.float32) * inv_root
    unstack(dq_ref, dq.astype(jnp.bfloat16))
    dv = tn(do, p_low).T
    dk = (tn(q, ds) * inv_root).T
    own_grad[:, pl.ds(at_key, HEAD_DIM)] = dk[:block]
    own_grad[:, pl.ds(at_value, HEAD_DIM)] = dv[:block]
    for k in range(1, count):
        piece = slice(k * block, (k + 1) * block)
        for at, grad in ((at_key, dk), (at_value, dv)):
            sent = grad[piece].astype(jnp.bfloat16)
            if opening:
                sent = jnp.where(place[0] >= k, sent, cols[k - 1][:, pl.ds(at, HEAD_DIM)])
            grads[k - 1][:, pl.ds(at, HEAD_DIM)] = sent


def attend(place, q, do, pairs, part, cols, before):
    block, width = q.shape
    count = len(pairs)
    steps = KV_HEADS // PARTS
    opening = not before

    def at_part(g, place):
        return (0, part * steps + g)

    wide = pl.BlockSpec((block, GROUP * HEAD_DIM), at_part)
    both = 2 * KV_WIDTH // PARTS
    rows = jax.ShapeDtypeStruct((block, width), jnp.bfloat16)
    own = pltpu.HBM((block, both), jnp.float32)
    sent = pltpu.VMEM((block, both), jnp.bfloat16)
    operands = [place, q, do, *(near(*pairs) if opening else far(*pairs))]
    in_specs = [wide, wide] + [vspec()] * count
    if opening:
        operands += near(*cols)
        in_specs += [vspec()] * (count - 1)
        out_specs = [wide, wide, vspec()] + [vspec()] * count
        out_shape = [rows, rows, pltpu.HBM((block, count * block), jnp.float32)]
        aliases = {}
    else:
        context, query_grad, mask = before
        aliases = {len(operands) + 1: 0, len(operands) + 2: 1}
        operands += [*far(mask), context, query_grad]
        in_specs += [vspec()] + [pl.BlockSpec(memory_space=pl.ANY)] * 2
        out_specs = [wide, wide] + [vspec()] * count
        out_shape = [rows, rows]
    outs = pl.pallas_call(
        functools.partial(attend_kernel, count=count, block=block, opening=opening),
        grid_spec=pltpu.PrefetchScalarGridSpec(
            num_scalar_prefetch=1, grid=(steps,), in_specs=in_specs, out_specs=out_specs
        ),
        out_shape=out_shape + [sent] * (count - 1) + [own],
        input_output_aliases=aliases,
        compiler_params=params(4 + 3 * count, dimension_semantics=("arbitrary",)),
        name="attend",
    )(*operands)
    return outs[: len(outs) - count], outs[len(outs) - count : -1], outs[-1]


def input_grad_kernel(place, *refs, count, rows):
    grads = refs[:PARTS]
    a_own, a_other, b_own, b_other, out, fa, fb = refs[PARTS:]
    half = KV_WIDTH // PARTS
    assemble(fa, a_own, a_other, place, count, rows)
    assemble(fb, b_own, b_other, place, count, rows)
    even = place[2] == 0
    gk = jnp.concatenate([g[:, :half] for g in grads], axis=1)
    gv = jnp.concatenate([g[:, half:] for g in grads], axis=1)
    ga = jnp.where(even, gk, gv)
    gb = jnp.where(even, gv, gk)
    out[...] = (nt(ga, fa[...]) + nt(gb, fb[...])).astype(jnp.bfloat16)


def input_grad_of(place, grads, a_own, a_other, b_own, b_other, count, rows):
    full = pltpu.VMEM((2 * count * rows, KV_WIDTH), jnp.bfloat16)
    operands = [*grads, a_own, a_other, b_own, b_other]
    return pl.pallas_call(
        functools.partial(input_grad_kernel, count=count, rows=rows),
        in_specs=[sspec()] + [vspec()] * len(operands),
        out_specs=vspec(),
        out_shape=jax.ShapeDtypeStruct((grads[0].shape[0], 2 * count * rows), jnp.bfloat16),
        scratch_shapes=[full, full],
        compiler_params=params(),
        name="input_grad",
    )(place, *near(*operands))


def turn_kernel(place, here, *refs, count, rows):
    wrapped, returned, out = refs[: count - 1], refs[count - 1 : 2 * count - 2], refs[-1]
    block = here.shape[0]
    for k in range(count):
        if k == 0:
            got = here[...]
        else:
            got = jnp.where(place[0] >= k, returned[count - k - 1][...], wrapped[k - 1][:block, :])
        for core in range(2):
            at = (2 * k + core) * block
            out[:, at : at + block] = got[:, core * rows : (core + 1) * rows].T


def turn(place, here, wrapped, returned, rows):
    count = len(wrapped) + 1
    return pl.pallas_call(
        functools.partial(turn_kernel, count=count, rows=rows),
        in_specs=[sspec()] + [vspec()] * (2 * count - 1),
        out_specs=vspec(),
        out_shape=pltpu.VMEM((rows, 2 * count * here.shape[0]), here.dtype),
        compiler_params=params(),
        name="turn",
    )(place, *near(here, *wrapped, *returned))


def weight_grad_kernel(x_turned, g_own, g_other, out, *, count):
    size = g_own.shape[0] // count
    pieces = []
    for k in range(count):
        pieces += [g_own[k * size : (k + 1) * size, :], g_other[k * size : (k + 1) * size, :]]
    grads = jnp.concatenate(pieces, axis=0)
    out[...] = jnp.dot(x_turned[...], grads, preferred_element_type=jnp.float32).astype(jnp.bfloat16)


def weight_grad_of(x_turned, g_own, g_other, count):
    return pl.pallas_call(
        functools.partial(weight_grad_kernel, count=count),
        in_specs=[vspec()] * 3,
        out_specs=vspec(),
        out_shape=pltpu.VMEM((x_turned.shape[0], g_own.shape[1]), jnp.bfloat16),
        compiler_params=params(),
        name="weight_grad",
    )(*near(x_turned, g_own, g_other))


def finish_kernel(place, *refs):
    pairs, outs = refs[:-2], refs[-2:]
    half = KV_WIDTH // PARTS
    for part in range(PARTS):
        a, b = pairs[2 * part], pairs[2 * part + 1]
        grad = (a[...].astype(jnp.float32) + b[...].astype(jnp.float32)).astype(jnp.bfloat16)
        outs[0][:, part * half : (part + 1) * half] = grad[:, :half]
        outs[1][:, part * half : (part + 1) * half] = grad[:, half:]


def finish(place, *partials):
    out = jax.ShapeDtypeStruct((partials[0].shape[0], KV_WIDTH), jnp.bfloat16)
    return pl.pallas_call(
        finish_kernel,
        in_specs=[sspec()] + [vspec()] * len(partials),
        out_specs=[vspec()] * 2,
        out_shape=[out, out],
        compiler_params=params(),
        name="finish",
    )(place, *near(*partials))


def body(activations, queries, key_weight, value_weight, segment_ids, out_grad):
    inputs = activations[0]
    block = inputs.shape[0]
    rows = key_weight.shape[0]
    n = lax.axis_size("seq")
    reps = lax.axis_size("rep")
    z, c = lax.axis_index("seq"), lax.axis_index("fsdp")
    odd = lax.rem(lax.axis_index("rep"), 2)
    place = jnp.stack([z, c, odd]).astype(jnp.int32)
    shifts = range(1, n)

    def around(x, k):
        return lax.ppermute(x, "seq", [(i, (i + k) % n) for i in range(n)])

    def up(x, k):
        return lax.ppermute(x, "seq", [(i, i + k) for i in range(n - k)])

    def down(x, k):
        return lax.ppermute(x, "seq", [(i, i - k) for i in range(k, n)])

    def pairwise(x, axis):
        return lax.ppermute(x, axis, [(j, j ^ 1) for j in range(lax.axis_size(axis))])

    def partner(x):
        return pairwise(x, "rep")

    def core(x):
        return pairwise(x, "fsdp")

    half = jnp.where(odd == 0, key_weight, value_weight)
    gathered = [half] + [around(half, k) for k in shifts]
    x_next = partner(inputs)
    x_for = cut(place, inputs, core(inputs), n, rows)
    gathered, x_next, x_for = lax.optimization_barrier((gathered, x_next, x_for))
    w_own = jnp.concatenate(gathered, axis=0)
    w_other = core(w_own)
    own, other = project(place, segment_ids, inputs, x_next, w_own, w_other, n, rows)
    pair, pair_2, loads = pack(place, own, partner(other), x_for[1:])
    carried = [around(x, k) for k, x in zip(shifts, loads)]
    ups = [up(pair_2, k) for k in shifts]

    queries, out_grad = queries[0], out_grad[0]
    before, sent_a, own_a = attend(
        place, queries, out_grad, [pair] + carried, 0, x_for[:0:-1], []
    )
    returned = [around(x, n - k) for k, x in zip(shifts, sent_a)]
    before, sent_b, own_b = attend(place, queries, out_grad, [pair_2] + ups, 1, [], before)
    sent_b, returned = lax.optimization_barrier((sent_b, returned))
    w_late, _ = lax.optimization_barrier((w_own, sent_b))
    b_own = partner(w_late)
    back_b = [down(x, k) for k, x in zip(shifts, sent_b)]
    back_a = [jnp.where(z + k < n, x, jnp.zeros_like(x)) for k, x in zip(shifts, returned)]
    sums = []
    for total, back in ((own_a, back_a), (own_b, back_b)):
        for x in back:
            total = total + x.astype(jnp.float32)
        sums.append(total.astype(jnp.bfloat16))
    context, query_grad = before[:2]
    x_turned = turn(place, x_for[0], carried, returned, rows)

    partials = []
    for part in range(PARTS):
        pieces = [sums[part]] + [around(sums[part], k) for k in shifts]
        if part == 0:
            pieces, _ = lax.optimization_barrier((pieces, sums[1]))
        else:
            pieces, partials, b_own = lax.optimization_barrier((pieces, partials, b_own))
            b_other = core(b_own)
        g_own = jnp.concatenate(pieces, axis=0)
        partials.append(weight_grad_of(x_turned, g_own, core(g_own), n))
    sums, _ = lax.optimization_barrier((sums, partials[-1]))
    input_grad = input_grad_of(place, sums, w_own, w_other, b_own, b_other, n, rows)
    if reps == 2:
        others = [partner(p) for p in partials]
        others, input_grad = lax.optimization_barrier((others, input_grad))
        grads = finish(place, *[x for p in zip(partials, others) for x in p])
    else:
        totals = [lax.psum(p.astype(jnp.float32), "rep").astype(jnp.bfloat16) for p in partials]
        grads = finish(place, *[x for p in totals for x in (p, jnp.zeros_like(p))])
    return context[None], query_grad[None], input_grad[None], grads[0], grads[1]


def solution(mesh):
    return jax.shard_map(
        body,
        mesh=mesh,
        in_specs=(
            P(("groups", "rep", "fsdp"), "seq", None),
            P(("groups", "rep", "fsdp"), "seq", None),
            P(("seq", "fsdp"), None),
            P(("seq", "fsdp"), None),
            P(("groups", "rep", "fsdp"), "seq"),
            P(("groups", "rep", "fsdp"), "seq", None),
        ),
        out_specs=(
            P(("groups", "rep", "fsdp"), "seq", None),
            P(("groups", "rep", "fsdp"), "seq", None),
            P(("groups", "rep", "fsdp"), "seq", None),
            P(("groups", "seq", "fsdp"), None),
            P(("groups", "seq", "fsdp"), None),
        ),
        check_vma=False,
    )
```

```python
import functools
import math

import jax
import jax.numpy as jnp
from jax import lax
from jax.experimental import pallas as pl
from jax.experimental.pallas import tpu as pltpu
from jax.sharding import PartitionSpec as P

HEADS = 16
KV_HEADS = 4
HEAD_DIM = 128
KV_WIDTH = KV_HEADS * HEAD_DIM
GROUP = HEADS // KV_HEADS
PARTS = 2
LOG2E = 1.4426950408889634
MASKED = -1e30
EXTRA = 16
LIGHT = pl.CostEstimate(flops=0, transcendentals=0, bytes_accessed=0)
MIB = 1024 * 1024


def far(*xs):
    return [pltpu.with_memory_space_constraint(x, pltpu.HBM) for x in xs]


def params(mib=16, **kw):
    return pltpu.CompilerParams(vmem_limit_bytes=mib * MIB, **kw)


def vspec():
    return pl.BlockSpec(memory_space=pltpu.VMEM)


def near(*xs):
    return [pltpu.with_memory_space_constraint(x, pltpu.VMEM) for x in xs]


def sspec():
    return pl.BlockSpec(memory_space=pltpu.SMEM)


def assemble(full_ref, own_ref, other_ref, place, count, rows):
    z, c = place[0], place[1]
    for k in range(count):
        src = lax.rem(z - k + count, count)
        for ref, core in ((own_ref, c), (other_ref, 1 - c)):
            start = pl.multiple_of((src * 2 + core) * rows, rows)
            full_ref[pl.ds(start, rows), :] = ref[k * rows : (k + 1) * rows, :]


def project_kernel(place, seg, x_own, x_next, w_own, w_other, out_own, out_next, full, *, count, rows):
    assemble(full, w_own, w_other, place, count, rows)
    w = full[...]
    block = x_own.shape[0]
    out_next[...] = jnp.dot(x_next[...], w, preferred_element_type=jnp.float32).astype(jnp.bfloat16)
    out_own[:block, :] = jnp.dot(x_own[...], w, preferred_element_type=jnp.float32).astype(
        jnp.bfloat16
    )
    ids = (seg[...] + 1).astype(jnp.float32)
    copies = out_own.shape[1] // block
    wide = jnp.concatenate([jnp.broadcast_to(ids, (EXTRA, block))] * copies, axis=1)
    out_own[block:, :] = wide.astype(jnp.bfloat16)


def project(place, seg, x_own, x_next, w_own, w_other, count, rows):
    width = w_own.shape[1]
    block = x_own.shape[0]
    return pl.pallas_call(
        functools.partial(project_kernel, count=count, rows=rows),
        in_specs=[sspec()] + [vspec()] * 5,
        out_specs=[vspec()] * 2,
        out_shape=[
            pltpu.VMEM((block + EXTRA, width), jnp.bfloat16),
            pltpu.VMEM((block, width), jnp.bfloat16),
        ],
        scratch_shapes=[pltpu.VMEM((2 * count * rows, width), jnp.bfloat16)],
        compiler_params=params(),
        name="project",
    )(place, seg, x_own, x_next, *near(w_own, w_other))


def cut_kernel(place, own, other, *outs, count, rows):
    for k in range(count):
        start = (lax.rem(place[0] + k, count) * 2 + place[1]) * rows
        start = pl.multiple_of(start, rows)
        outs[k][:, :rows] = own[:, pl.ds(start, rows)]
        outs[k][:, rows:] = other[:, pl.ds(start, rows)]


def cut(place, own, other, count, rows):
    block = own.shape[0]
    if rows % 128 or 2 * rows != KV_WIDTH:
        pieces = []
        for k in range(count):
            start = (lax.rem(place[0] + k, count) * 2 + place[1]) * rows
            both = [lax.dynamic_slice_in_dim(x, start, rows, 1) for x in (own, other)]
            wide = jnp.concatenate(both, axis=1)
            pieces.append(jnp.pad(wide, ((0, 0), (0, KV_WIDTH - 2 * rows))))
        return pieces
    return pl.pallas_call(
        functools.partial(cut_kernel, count=count, rows=rows),
        in_specs=[sspec()] + [vspec()] * 2,
        out_specs=[vspec()] * count,
        out_shape=[pltpu.VMEM((block, 2 * rows), own.dtype)] * count,
        compiler_params=params(),
        name="cut",
    )(place, own, *near(other))


def pack_kernel(place, own, mate, *refs, count):
    cols, outs = refs[: count - 1], refs[count - 1 :]
    block, width = mate.shape
    half = width // PARTS
    first = jnp.concatenate([own[:block, :half], mate[:, :half]], axis=1)
    tail = own[block:, :]
    outs[0][:block, :] = first
    outs[0][block:, :] = tail
    outs[1][...] = jnp.concatenate([own[:block, half:], mate[:, half:]], axis=1)
    for k in range(1, count):
        goes_up = place[0] + k < count
        outs[k + 1][:block, :] = jnp.where(goes_up, first, cols[k - 1][...])
        outs[k + 1][block:, :] = jnp.where(goes_up, tail, jnp.zeros_like(tail))


def pack(place, own, mate, cols):
    count = len(cols) + 1
    tall = pltpu.VMEM(own.shape, own.dtype)
    outs = pl.pallas_call(
        functools.partial(pack_kernel, count=count),
        in_specs=[sspec()] + [vspec()] * (count + 1),
        out_specs=[vspec()] * (count + 1),
        out_shape=[tall, pltpu.VMEM(mate.shape, mate.dtype)] + [tall] * (count - 1),
        compiler_params=params(),
        name="pack",
    )(place, *near(own, mate, *cols))
    return outs[0], outs[1], outs[2:]


def nt(a, b):
    return lax.dot_general(a, b, (((1,), (1,)), ((), ())), preferred_element_type=jnp.float32)


def tn(a, b):
    return lax.dot_general(a, b, (((0,), (0,)), ((), ())), preferred_element_type=jnp.float32)


def attend_kernel(place, q_ref, do_ref, *refs, count, block, opening):
    pair_refs, refs = refs[:count], refs[count:]
    if opening:
        cols = refs[: count - 1]
        ctx_ref, dq_ref, bias = refs[count - 1 : count + 2]
        grads, own_grad = refs[count + 2 : -1], refs[-1]
    else:
        bias = refs[0]
        ctx_ref, dq_ref = refs[3:5]
        grads, own_grad = refs[5:-1], refs[-1]
    inv_root = 1.0 / math.sqrt(HEAD_DIM)
    length = count * block

    if opening:

        @pl.when(pl.program_id(0) == 0)
        def _():
            ids = [r[block : block + 1, :block].astype(jnp.float32) for r in pair_refs]
            mine = jnp.broadcast_to(ids[0], (block, block)).T
            rows = lax.broadcasted_iota(jnp.int32, (block, block), 0)
            cols_here = lax.broadcasted_iota(jnp.int32, (block, block), 1)
            for k in range(count):
                ok = mine == jnp.broadcast_to(ids[k], (block, block))
                if k == 0:
                    ok = ok & (cols_here <= rows)
                bias[:, k * block : (k + 1) * block] = jnp.where(ok, 0.0, MASKED)

    even = place[2] == 0
    at_key = pl.multiple_of(pl.program_id(0) * HEAD_DIM, HEAD_DIM)
    at_value = pl.multiple_of(at_key + KV_WIDTH // PARTS, HEAD_DIM)
    a = jnp.concatenate([r[:block, pl.ds(at_key, HEAD_DIM)] for r in pair_refs], axis=0)
    b = jnp.concatenate([r[:block, pl.ds(at_value, HEAD_DIM)] for r in pair_refs], axis=0)
    key = jnp.where(even, a, b)
    value = jnp.where(even, b, a)

    def stack(ref):
        return jnp.concatenate(
            [ref[:, h * HEAD_DIM : (h + 1) * HEAD_DIM] for h in range(GROUP)], axis=0
        )

    def unstack(ref, val):
        for h in range(GROUP):
            ref[:, h * HEAD_DIM : (h + 1) * HEAD_DIM] = val[h * block : (h + 1) * block, :]

    q, do = stack(q_ref), stack(do_ref)
    s = nt(q, key) * (inv_root * LOG2E)
    s = (s.reshape(GROUP, block, length) + bias[...][None]).reshape(GROUP * block, length)
    e = jnp.exp2(s - jnp.max(s, axis=1, keepdims=True))
    p = e * (1.0 / jnp.sum(e, axis=1, keepdims=True))
    p_low = p.astype(jnp.bfloat16)
    ctx = jnp.dot(p_low, value, preferred_element_type=jnp.float32).astype(jnp.bfloat16)
    unstack(ctx_ref, ctx)
    dots = jnp.sum(do.astype(jnp.float32) * ctx.astype(jnp.float32), axis=1, keepdims=True)
    ds = (p * (nt(do, value) - dots)).astype(jnp.bfloat16)
    dq = jnp.dot(ds, key, preferred_element_type=jnp.float32) * inv_root
    unstack(dq_ref, dq.astype(jnp.bfloat16))
    dv = tn(do, p_low).T
    dk = (tn(q, ds) * inv_root).T
    own_grad[:, pl.ds(at_key, HEAD_DIM)] = dk[:block]
    own_grad[:, pl.ds(at_value, HEAD_DIM)] = dv[:block]
    for k in range(1, count):
        piece = slice(k * block, (k + 1) * block)
        for at, grad in ((at_key, dk), (at_value, dv)):
            sent = grad[piece].astype(jnp.bfloat16)
            if opening:
                sent = jnp.where(place[0] >= k, sent, cols[k - 1][:, pl.ds(at, HEAD_DIM)])
            grads[k - 1][:, pl.ds(at, HEAD_DIM)] = sent


def attend(place, q, do, pairs, part, cols, before):
    block, width = q.shape
    count = len(pairs)
    steps = KV_HEADS // PARTS
    opening = not before

    def at_part(g, place):
        return (0, part * steps + g)

    wide = pl.BlockSpec((block, GROUP * HEAD_DIM), at_part)
    both = 2 * KV_WIDTH // PARTS
    rows = jax.ShapeDtypeStruct((block, width), jnp.bfloat16)
    own = pltpu.HBM((block, both), jnp.float32)
    sent = pltpu.VMEM((block, both), jnp.bfloat16)
    operands = [place, q, do, *(near(*pairs) if opening else far(*pairs))]
    in_specs = [wide, wide] + [vspec()] * count
    if opening:
        operands += near(*cols)
        in_specs += [vspec()] * (count - 1)
        out_specs = [wide, wide, vspec()] + [vspec()] * count
        out_shape = [rows, rows, pltpu.HBM((block, count * block), jnp.float32)]
        aliases = {}
    else:
        context, query_grad, mask = before
        aliases = {len(operands) + 1: 0, len(operands) + 2: 1}
        operands += [*far(mask), context, query_grad]
        in_specs += [vspec()] + [pl.BlockSpec(memory_space=pl.ANY)] * 2
        out_specs = [wide, wide] + [vspec()] * count
        out_shape = [rows, rows]
    outs = pl.pallas_call(
        functools.partial(attend_kernel, count=count, block=block, opening=opening),
        grid_spec=pltpu.PrefetchScalarGridSpec(
            num_scalar_prefetch=1, grid=(steps,), in_specs=in_specs, out_specs=out_specs
        ),
        out_shape=out_shape + [sent] * (count - 1) + [own],
        input_output_aliases=aliases,
        compiler_params=params(4 + 3 * count, dimension_semantics=("arbitrary",)),
        name="attend",
    )(*operands)
    return outs[: len(outs) - count], outs[len(outs) - count : -1], outs[-1]


def input_grad_kernel(place, *refs, count, rows):
    grads = refs[:PARTS]
    a_own, a_other, b_own, b_other, out, fa, fb = refs[PARTS:]
    half = KV_WIDTH // PARTS
    assemble(fa, a_own, a_other, place, count, rows)
    assemble(fb, b_own, b_other, place, count, rows)
    even = place[2] == 0
    gk = jnp.concatenate([g[:, :half] for g in grads], axis=1)
    gv = jnp.concatenate([g[:, half:] for g in grads], axis=1)
    ga = jnp.where(even, gk, gv)
    gb = jnp.where(even, gv, gk)
    out[...] = (nt(ga, fa[...]) + nt(gb, fb[...])).astype(jnp.bfloat16)


def input_grad_of(place, grads, a_own, a_other, b_own, b_other, count, rows):
    full = pltpu.VMEM((2 * count * rows, KV_WIDTH), jnp.bfloat16)
    operands = [*grads, a_own, a_other, b_own, b_other]
    return pl.pallas_call(
        functools.partial(input_grad_kernel, count=count, rows=rows),
        in_specs=[sspec()] + [vspec()] * len(operands),
        out_specs=vspec(),
        out_shape=jax.ShapeDtypeStruct((grads[0].shape[0], 2 * count * rows), jnp.bfloat16),
        scratch_shapes=[full, full],
        compiler_params=params(),
        name="input_grad",
    )(place, *near(*operands))


def turn_kernel(place, here, *refs, count, rows):
    wrapped, returned, out = refs[: count - 1], refs[count - 1 : 2 * count - 2], refs[-1]
    block = here.shape[0]
    for k in range(count):
        if k == 0:
            got = here[...]
        else:
            got = jnp.where(place[0] >= k, returned[count - k - 1][...], wrapped[k - 1][:block, :])
        for core in range(2):
            at = (2 * k + core) * block
            out[:, at : at + block] = got[:, core * rows : (core + 1) * rows].T


def turn(place, here, wrapped, returned, rows):
    count = len(wrapped) + 1
    return pl.pallas_call(
        functools.partial(turn_kernel, count=count, rows=rows),
        in_specs=[sspec()] + [vspec()] * (2 * count - 1),
        out_specs=vspec(),
        out_shape=pltpu.VMEM((rows, 2 * count * here.shape[0]), here.dtype),
        compiler_params=params(),
        name="turn",
    )(place, *near(here, *wrapped, *returned))


def weight_grad_kernel(x_turned, g_own, g_other, out, *, count):
    size = g_own.shape[0] // count
    pieces = []
    for k in range(count):
        pieces += [g_own[k * size : (k + 1) * size, :], g_other[k * size : (k + 1) * size, :]]
    grads = jnp.concatenate(pieces, axis=0)
    out[...] = jnp.dot(x_turned[...], grads, preferred_element_type=jnp.float32).astype(jnp.bfloat16)


def weight_grad_of(x_turned, g_own, g_other, count):
    return pl.pallas_call(
        functools.partial(weight_grad_kernel, count=count),
        in_specs=[vspec()] * 3,
        out_specs=vspec(),
        out_shape=pltpu.VMEM((x_turned.shape[0], g_own.shape[1]), jnp.bfloat16),
        compiler_params=params(),
        name="weight_grad",
    )(*near(x_turned, g_own, g_other))


def finish_kernel(place, *refs):
    pairs, outs = refs[:-2], refs[-2:]
    half = KV_WIDTH // PARTS
    for part in range(PARTS):
        a, b = pairs[2 * part], pairs[2 * part + 1]
        grad = (a[...].astype(jnp.float32) + b[...].astype(jnp.float32)).astype(jnp.bfloat16)
        outs[0][:, part * half : (part + 1) * half] = grad[:, :half]
        outs[1][:, part * half : (part + 1) * half] = grad[:, half:]


def finish(place, *partials):
    out = jax.ShapeDtypeStruct((partials[0].shape[0], KV_WIDTH), jnp.bfloat16)
    return pl.pallas_call(
        finish_kernel,
        in_specs=[sspec()] + [vspec()] * len(partials),
        out_specs=[vspec()] * 2,
        out_shape=[out, out],
        compiler_params=params(),
        name="finish",
    )(place, *near(*partials))


def body(activations, queries, key_weight, value_weight, segment_ids, out_grad):
    inputs = activations[0]
    block = inputs.shape[0]
    rows = key_weight.shape[0]
    n = lax.axis_size("seq")
    reps = lax.axis_size("rep")
    z, c = lax.axis_index("seq"), lax.axis_index("fsdp")
    odd = lax.rem(lax.axis_index("rep"), 2)
    place = jnp.stack([z, c, odd]).astype(jnp.int32)
    shifts = range(1, n)

    def around(x, k):
        return lax.ppermute(x, "seq", [(i, (i + k) % n) for i in range(n)])

    def up(x, k):
        return lax.ppermute(x, "seq", [(i, i + k) for i in range(n - k)])

    def down(x, k):
        return lax.ppermute(x, "seq", [(i, i - k) for i in range(k, n)])

    def pairwise(x, axis):
        return lax.ppermute(x, axis, [(j, j ^ 1) for j in range(lax.axis_size(axis))])

    def partner(x):
        return pairwise(x, "rep")

    def core(x):
        return pairwise(x, "fsdp")

    half = jnp.where(odd == 0, key_weight, value_weight)
    gathered = [half] + [around(half, k) for k in shifts]
    x_next = partner(inputs)
    x_for = cut(place, inputs, core(inputs), n, rows)
    gathered, x_next, x_for = lax.optimization_barrier((gathered, x_next, x_for))
    w_own = jnp.concatenate(gathered, axis=0)
    w_other = core(w_own)
    own, other = project(place, segment_ids, inputs, x_next, w_own, w_other, n, rows)
    pair, pair_2, loads = pack(place, own, partner(other), x_for[1:])
    carried = [around(x, k) for k, x in zip(shifts, loads)]
    ups = [up(pair_2, k) for k in shifts]

    queries, out_grad = queries[0], out_grad[0]
    before, sent_a, own_a = attend(
        place, queries, out_grad, [pair] + carried, 0, x_for[:0:-1], []
    )
    returned = [around(x, n - k) for k, x in zip(shifts, sent_a)]
    before, sent_b, own_b = attend(place, queries, out_grad, [pair_2] + ups, 1, [], before)
    sent_b, returned = lax.optimization_barrier((sent_b, returned))
    w_late, _ = lax.optimization_barrier((w_own, sent_b))
    b_own = partner(w_late)
    back_b = [down(x, k) for k, x in zip(shifts, sent_b)]
    back_a = [jnp.where(z + k < n, x, jnp.zeros_like(x)) for k, x in zip(shifts, returned)]
    sums = []
    for total, back in ((own_a, back_a), (own_b, back_b)):
        for x in back:
            total = total + x.astype(jnp.float32)
        sums.append(total.astype(jnp.bfloat16))
    context, query_grad = before[:2]
    x_turned = turn(place, x_for[0], carried, returned, rows)

    def over_reps(x):
        if reps == 2:
            return [x, partner(x)]
        return [lax.psum(x.astype(jnp.float32), "rep").astype(x.dtype), jnp.zeros_like(x)]

    finals = []
    for part in range(PARTS):
        pieces = [sums[part]] + [around(sums[part], k) for k in shifts]
        if part == 0:
            pieces, _ = lax.optimization_barrier((pieces, sums[1]))
        else:
            pieces, b_own = lax.optimization_barrier((pieces, b_own))
            b_other = core(b_own)
        g_own = jnp.concatenate(pieces, axis=0)
        g_own, finals = lax.optimization_barrier((g_own, finals))
        partial = weight_grad_of(x_turned, g_own, core(g_own), n)
        finals += over_reps(partial)
    sums, _ = lax.optimization_barrier((sums, partial))
    input_grad = input_grad_of(place, sums, w_own, w_other, b_own, b_other, n, rows)
    finals, input_grad = lax.optimization_barrier((finals, input_grad))
    grads = finish(place, *finals)
    return context[None], query_grad[None], input_grad[None], grads[0], grads[1]


def solution(mesh):
    return jax.shard_map(
        body,
        mesh=mesh,
        in_specs=(
            P(("groups", "rep", "fsdp"), "seq", None),
            P(("groups", "rep", "fsdp"), "seq", None),
            P(("seq", "fsdp"), None),
            P(("seq", "fsdp"), None),
            P(("groups", "rep", "fsdp"), "seq"),
            P(("groups", "rep", "fsdp"), "seq", None),
        ),
        out_specs=(
            P(("groups", "rep", "fsdp"), "seq", None),
            P(("groups", "rep", "fsdp"), "seq", None),
            P(("groups", "rep", "fsdp"), "seq", None),
            P(("groups", "seq", "fsdp"), None),
            P(("groups", "seq", "fsdp"), None),
        ),
        check_vma=False,
    )
```

```python
import functools
import math

import jax
import jax.numpy as jnp
from jax import lax
from jax.experimental import pallas as pl
from jax.experimental.pallas import tpu as pltpu
from jax.sharding import PartitionSpec as P

HEADS = 16
KV_HEADS = 4
HEAD_DIM = 128
KV_WIDTH = KV_HEADS * HEAD_DIM
GROUP = HEADS // KV_HEADS
PARTS = 2
LOG2E = 1.4426950408889634
MASKED = -1e30
EXTRA = 16
LIGHT = pl.CostEstimate(flops=0, transcendentals=0, bytes_accessed=0)
MIB = 1024 * 1024


def far(*xs):
    return [pltpu.with_memory_space_constraint(x, pltpu.HBM) for x in xs]


def params(mib=16, **kw):
    return pltpu.CompilerParams(vmem_limit_bytes=mib * MIB, **kw)


def vspec():
    return pl.BlockSpec(memory_space=pltpu.VMEM)


def near(*xs):
    return [pltpu.with_memory_space_constraint(x, pltpu.VMEM) for x in xs]


def sspec():
    return pl.BlockSpec(memory_space=pltpu.SMEM)


def assemble(full_ref, own_ref, other_ref, place, count, rows):
    z, c = place[0], place[1]
    for k in range(count):
        src = lax.rem(z - k + count, count)
        for ref, core in ((own_ref, c), (other_ref, 1 - c)):
            start = pl.multiple_of((src * 2 + core) * rows, rows)
            full_ref[pl.ds(start, rows), :] = ref[k * rows : (k + 1) * rows, :]


def project_kernel(place, seg, x_own, x_next, w_own, w_other, out_own, out_next, full, *, count, rows):
    assemble(full, w_own, w_other, place, count, rows)
    w = full[...]
    block = x_own.shape[0]
    out_next[...] = jnp.dot(x_next[...], w, preferred_element_type=jnp.float32).astype(jnp.bfloat16)
    out_own[:block, :] = jnp.dot(x_own[...], w, preferred_element_type=jnp.float32).astype(
        jnp.bfloat16
    )
    ids = (seg[...] + 1).astype(jnp.float32)
    copies = out_own.shape[1] // block
    wide = jnp.concatenate([jnp.broadcast_to(ids, (EXTRA, block))] * copies, axis=1)
    out_own[block:, :] = wide.astype(jnp.bfloat16)


def project(place, seg, x_own, x_next, w_own, w_other, count, rows):
    width = w_own.shape[1]
    block = x_own.shape[0]
    return pl.pallas_call(
        functools.partial(project_kernel, count=count, rows=rows),
        in_specs=[sspec()] + [vspec()] * 5,
        out_specs=[vspec()] * 2,
        out_shape=[
            pltpu.VMEM((block + EXTRA, width), jnp.bfloat16),
            pltpu.VMEM((block, width), jnp.bfloat16),
        ],
        scratch_shapes=[pltpu.VMEM((2 * count * rows, width), jnp.bfloat16)],
        compiler_params=params(),
        name="project",
    )(place, seg, x_own, x_next, *near(w_own, w_other))


def cut_kernel(place, own, other, *outs, count, rows):
    for k in range(count):
        start = (lax.rem(place[0] + k, count) * 2 + place[1]) * rows
        start = pl.multiple_of(start, rows)
        outs[k][:, :rows] = own[:, pl.ds(start, rows)]
        outs[k][:, rows:] = other[:, pl.ds(start, rows)]


def cut(place, own, other, count, rows):
    block = own.shape[0]
    if rows % 128 or 2 * rows != KV_WIDTH:
        pieces = []
        for k in range(count):
            start = (lax.rem(place[0] + k, count) * 2 + place[1]) * rows
            both = [lax.dynamic_slice_in_dim(x, start, rows, 1) for x in (own, other)]
            wide = jnp.concatenate(both, axis=1)
            pieces.append(jnp.pad(wide, ((0, 0), (0, KV_WIDTH - 2 * rows))))
        return pieces
    return pl.pallas_call(
        functools.partial(cut_kernel, count=count, rows=rows),
        in_specs=[sspec()] + [vspec()] * 2,
        out_specs=[vspec()] * count,
        out_shape=[pltpu.VMEM((block, 2 * rows), own.dtype)] * count,
        compiler_params=params(),
        name="cut",
    )(place, own, *near(other))


def pack_kernel(place, own, mate, *refs, count):
    cols, outs = refs[: count - 1], refs[count - 1 :]
    block, width = mate.shape
    half = width // PARTS
    first = jnp.concatenate([own[:block, :half], mate[:, :half]], axis=1)
    tail = own[block:, :]
    outs[0][:block, :] = first
    outs[0][block:, :] = tail
    outs[1][...] = jnp.concatenate([own[:block, half:], mate[:, half:]], axis=1)
    for k in range(1, count):
        goes_up = place[0] + k < count
        outs[k + 1][:block, :] = jnp.where(goes_up, first, cols[k - 1][...])
        outs[k + 1][block:, :] = jnp.where(goes_up, tail, jnp.zeros_like(tail))


def pack(place, own, mate, cols):
    count = len(cols) + 1
    tall = pltpu.VMEM(own.shape, own.dtype)
    outs = pl.pallas_call(
        functools.partial(pack_kernel, count=count),
        in_specs=[sspec()] + [vspec()] * (count + 1),
        out_specs=[vspec()] * (count + 1),
        out_shape=[tall, pltpu.VMEM(mate.shape, mate.dtype)] + [tall] * (count - 1),
        compiler_params=params(),
        name="pack",
    )(place, *near(own, mate, *cols))
    return outs[0], outs[1], outs[2:]


def nt(a, b):
    return lax.dot_general(a, b, (((1,), (1,)), ((), ())), preferred_element_type=jnp.float32)


def tn(a, b):
    return lax.dot_general(a, b, (((0,), (0,)), ((), ())), preferred_element_type=jnp.float32)


def attend_kernel(place, q_ref, do_ref, *refs, count, block, opening):
    pair_refs, refs = refs[:count], refs[count:]
    if not opening:
        value_refs, refs = refs[:count], refs[count:]
    if opening:
        cols = refs[: count - 1]
        ctx_ref, dq_ref, bias = refs[count - 1 : count + 2]
        grads, own_grad = refs[count + 2 : -1], refs[-1]
    else:
        bias = refs[0]
        ctx_ref, dq_ref = refs[3:5]
        grads, own_grad = refs[5:-1], refs[-1]
    inv_root = 1.0 / math.sqrt(HEAD_DIM)
    length = count * block

    if opening:

        @pl.when(pl.program_id(0) == 0)
        def _():
            ids = [r[block : block + 1, :block].astype(jnp.float32) for r in pair_refs]
            mine = jnp.broadcast_to(ids[0], (block, block)).T
            rows = lax.broadcasted_iota(jnp.int32, (block, block), 0)
            cols_here = lax.broadcasted_iota(jnp.int32, (block, block), 1)
            for k in range(count):
                ok = mine == jnp.broadcast_to(ids[k], (block, block))
                if k == 0:
                    ok = ok & (cols_here <= rows)
                bias[:, k * block : (k + 1) * block] = jnp.where(ok, 0.0, MASKED)

    even = place[2] == 0
    at_key = pl.multiple_of(pl.program_id(0) * HEAD_DIM, HEAD_DIM)
    at_value = pl.multiple_of(at_key + KV_WIDTH // PARTS, HEAD_DIM)
    if opening:
        a = [r[:block, pl.ds(at_key, HEAD_DIM)] for r in pair_refs]
        b = [r[:block, pl.ds(at_value, HEAD_DIM)] for r in pair_refs]
    else:
        a, b = [r[...] for r in pair_refs], [r[...] for r in value_refs]
    a, b = jnp.concatenate(a, axis=0), jnp.concatenate(b, axis=0)
    key = jnp.where(even, a, b)
    value = jnp.where(even, b, a)

    def stack(ref):
        return jnp.concatenate(
            [ref[:, h * HEAD_DIM : (h + 1) * HEAD_DIM] for h in range(GROUP)], axis=0
        )

    def unstack(ref, val):
        for h in range(GROUP):
            ref[:, h * HEAD_DIM : (h + 1) * HEAD_DIM] = val[h * block : (h + 1) * block, :]

    q, do = stack(q_ref), stack(do_ref)
    s = nt(q, key) * (inv_root * LOG2E)
    s = (s.reshape(GROUP, block, length) + bias[...][None]).reshape(GROUP * block, length)
    e = jnp.exp2(s - jnp.max(s, axis=1, keepdims=True))
    p = e * (1.0 / jnp.sum(e, axis=1, keepdims=True))
    p_low = p.astype(jnp.bfloat16)
    ctx = jnp.dot(p_low, value, preferred_element_type=jnp.float32).astype(jnp.bfloat16)
    unstack(ctx_ref, ctx)
    dots = jnp.sum(do.astype(jnp.float32) * ctx.astype(jnp.float32), axis=1, keepdims=True)
    ds = (p * (nt(do, value) - dots)).astype(jnp.bfloat16)
    dq = jnp.dot(ds, key, preferred_element_type=jnp.float32) * inv_root
    unstack(dq_ref, dq.astype(jnp.bfloat16))
    dv = tn(do, p_low).T
    dk = (tn(q, ds) * inv_root).T
    own_grad[:, pl.ds(at_key, HEAD_DIM)] = dk[:block]
    own_grad[:, pl.ds(at_value, HEAD_DIM)] = dv[:block]
    for k in range(1, count):
        piece = slice(k * block, (k + 1) * block)
        for at, grad in ((at_key, dk), (at_value, dv)):
            sent = grad[piece].astype(jnp.bfloat16)
            if opening:
                sent = jnp.where(place[0] >= k, sent, cols[k - 1][:, pl.ds(at, HEAD_DIM)])
            grads[k - 1][:, pl.ds(at, HEAD_DIM)] = sent


def attend(place, q, do, pairs, part, cols, before):
    block, width = q.shape
    count = len(pairs)
    steps = KV_HEADS // PARTS
    opening = not before

    def at_part(g, place):
        return (0, part * steps + g)

    wide = pl.BlockSpec((block, GROUP * HEAD_DIM), at_part)
    both = 2 * KV_WIDTH // PARTS
    rows = jax.ShapeDtypeStruct((block, width), jnp.bfloat16)
    own = pltpu.HBM((block, both), jnp.float32)
    sent = pltpu.VMEM((block, both), jnp.bfloat16)
    operands = [place, q, do, *(near(*pairs) if opening else far(*pairs))]
    in_specs = [wide, wide] + [vspec()] * count
    if opening:
        operands += near(*cols)
        in_specs += [vspec()] * (count - 1)
        out_specs = [wide, wide, vspec()] + [vspec()] * count
        out_shape = [rows, rows, pltpu.HBM((block, count * block), jnp.float32)]
        aliases = {}
    else:
        context, query_grad, mask = before
        operands += far(*pairs)
        in_specs = [wide, wide]
        in_specs += [pl.BlockSpec((block, HEAD_DIM), lambda g, place: (0, g))] * count
        in_specs += [pl.BlockSpec((block, HEAD_DIM), lambda g, place: (0, steps + g))] * count
        aliases = {len(operands) + 1: 0, len(operands) + 2: 1}
        operands += [*far(mask), context, query_grad]
        in_specs += [pl.BlockSpec((block, count * block), lambda g, place: (0, 0))]
        in_specs += [pl.BlockSpec(memory_space=pl.ANY)] * 2
        out_specs = [wide, wide] + [vspec()] * count
        out_shape = [rows, rows]
    outs = pl.pallas_call(
        functools.partial(attend_kernel, count=count, block=block, opening=opening),
        grid_spec=pltpu.PrefetchScalarGridSpec(
            num_scalar_prefetch=1, grid=(steps,), in_specs=in_specs, out_specs=out_specs
        ),
        out_shape=out_shape + [sent] * (count - 1) + [own],
        input_output_aliases=aliases,
        compiler_params=params(4 + 3 * count, dimension_semantics=("arbitrary",)),
        name="attend",
    )(*operands)
    return outs[: len(outs) - count], outs[len(outs) - count : -1], outs[-1]


def input_grad_kernel(place, *refs, count, rows):
    grads = refs[:PARTS]
    a_own, a_other, b_own, b_other, out, fa, fb = refs[PARTS:]
    half = KV_WIDTH // PARTS
    assemble(fa, a_own, a_other, place, count, rows)
    assemble(fb, b_own, b_other, place, count, rows)
    even = place[2] == 0
    gk = jnp.concatenate([g[:, :half] for g in grads], axis=1)
    gv = jnp.concatenate([g[:, half:] for g in grads], axis=1)
    ga = jnp.where(even, gk, gv)
    gb = jnp.where(even, gv, gk)
    out[...] = (nt(ga, fa[...]) + nt(gb, fb[...])).astype(jnp.bfloat16)


def input_grad_of(place, grads, a_own, a_other, b_own, b_other, count, rows):
    full = pltpu.VMEM((2 * count * rows, KV_WIDTH), jnp.bfloat16)
    operands = [*grads, a_own, a_other, b_own, b_other]
    return pl.pallas_call(
        functools.partial(input_grad_kernel, count=count, rows=rows),
        in_specs=[sspec()] + [vspec()] * len(operands),
        out_specs=vspec(),
        out_shape=jax.ShapeDtypeStruct((grads[0].shape[0], 2 * count * rows), jnp.bfloat16),
        scratch_shapes=[full, full],
        compiler_params=params(),
        name="input_grad",
    )(place, *near(*operands))


def turn_kernel(place, here, *refs, count, rows):
    wrapped, returned, out = refs[: count - 1], refs[count - 1 : 2 * count - 2], refs[-1]
    block = here.shape[0]
    for k in range(count):
        if k == 0:
            got = here[...]
        else:
            got = jnp.where(place[0] >= k, returned[count - k - 1][...], wrapped[k - 1][:block, :])
        for core in range(2):
            at = (2 * k + core) * block
            out[:, at : at + block] = got[:, core * rows : (core + 1) * rows].T


def turn(place, here, wrapped, returned, rows):
    count = len(wrapped) + 1
    return pl.pallas_call(
        functools.partial(turn_kernel, count=count, rows=rows),
        in_specs=[sspec()] + [vspec()] * (2 * count - 1),
        out_specs=vspec(),
        out_shape=pltpu.VMEM((rows, 2 * count * here.shape[0]), here.dtype),
        compiler_params=params(),
        name="turn",
    )(place, *near(here, *wrapped, *returned))


def weight_grad_kernel(x_turned, g_own, g_other, out, *, count):
    size = g_own.shape[0] // count
    pieces = []
    for k in range(count):
        pieces += [g_own[k * size : (k + 1) * size, :], g_other[k * size : (k + 1) * size, :]]
    grads = jnp.concatenate(pieces, axis=0)
    out[...] = jnp.dot(x_turned[...], grads, preferred_element_type=jnp.float32).astype(jnp.bfloat16)


def weight_grad_of(x_turned, g_own, g_other, count):
    return pl.pallas_call(
        functools.partial(weight_grad_kernel, count=count),
        in_specs=[vspec()] * 3,
        out_specs=vspec(),
        out_shape=pltpu.VMEM((x_turned.shape[0], g_own.shape[1]), jnp.bfloat16),
        compiler_params=params(),
        name="weight_grad",
    )(*near(x_turned, g_own, g_other))


def finish_kernel(place, *refs):
    pairs, outs = refs[:-2], refs[-2:]
    half = KV_WIDTH // PARTS
    for part in range(PARTS):
        a, b = pairs[2 * part], pairs[2 * part + 1]
        grad = (a[...].astype(jnp.float32) + b[...].astype(jnp.float32)).astype(jnp.bfloat16)
        outs[0][:, part * half : (part + 1) * half] = grad[:, :half]
        outs[1][:, part * half : (part + 1) * half] = grad[:, half:]


def finish(place, *partials):
    out = jax.ShapeDtypeStruct((partials[0].shape[0], KV_WIDTH), jnp.bfloat16)
    return pl.pallas_call(
        finish_kernel,
        in_specs=[sspec()] + [vspec()] * len(partials),
        out_specs=[vspec()] * 2,
        out_shape=[out, out],
        compiler_params=params(),
        name="finish",
    )(place, *near(*partials))


def body(activations, queries, key_weight, value_weight, segment_ids, out_grad):
    inputs = activations[0]
    block = inputs.shape[0]
    rows = key_weight.shape[0]
    n = lax.axis_size("seq")
    reps = lax.axis_size("rep")
    z, c = lax.axis_index("seq"), lax.axis_index("fsdp")
    odd = lax.rem(lax.axis_index("rep"), 2)
    place = jnp.stack([z, c, odd]).astype(jnp.int32)
    shifts = range(1, n)

    def around(x, k):
        return lax.ppermute(x, "seq", [(i, (i + k) % n) for i in range(n)])

    def up(x, k):
        return lax.ppermute(x, "seq", [(i, i + k) for i in range(n - k)])

    def down(x, k):
        return lax.ppermute(x, "seq", [(i, i - k) for i in range(k, n)])

    def pairwise(x, axis):
        return lax.ppermute(x, axis, [(j, j ^ 1) for j in range(lax.axis_size(axis))])

    def partner(x):
        return pairwise(x, "rep")

    def core(x):
        return pairwise(x, "fsdp")

    half = jnp.where(odd == 0, key_weight, value_weight)
    gathered = [half] + [around(half, k) for k in shifts]
    x_next = partner(inputs)
    x_for = cut(place, inputs, core(inputs), n, rows)
    gathered, x_next, x_for = lax.optimization_barrier((gathered, x_next, x_for))
    w_own = jnp.concatenate(gathered, axis=0)
    w_other = core(w_own)
    own, other = project(place, segment_ids, inputs, x_next, w_own, w_other, n, rows)
    pair, pair_2, loads = pack(place, own, partner(other), x_for[1:])
    carried = [around(x, k) for k, x in zip(shifts, loads)]
    ups = [up(pair_2, k) for k in shifts]

    queries, out_grad = queries[0], out_grad[0]
    before, sent_a, own_a = attend(
        place, queries, out_grad, [pair] + carried, 0, x_for[:0:-1], []
    )
    returned = [around(x, n - k) for k, x in zip(shifts, sent_a)]
    before, sent_b, own_b = attend(place, queries, out_grad, [pair_2] + ups, 1, [], before)
    sent_b, returned = lax.optimization_barrier((sent_b, returned))
    w_late, _ = lax.optimization_barrier((w_own, sent_b))
    b_own = partner(w_late)
    back_b = [down(x, k) for k, x in zip(shifts, sent_b)]
    back_a = [jnp.where(z + k < n, x, jnp.zeros_like(x)) for k, x in zip(shifts, returned)]
    sums = []
    for total, back in ((own_a, back_a), (own_b, back_b)):
        for x in back:
            total = total + x.astype(jnp.float32)
        sums.append(total.astype(jnp.bfloat16))
    context, query_grad = before[:2]
    x_turned = turn(place, x_for[0], carried, returned, rows)

    def over_reps(x):
        if reps == 2:
            return [x, partner(x)]
        return [lax.psum(x.astype(jnp.float32), "rep").astype(x.dtype), jnp.zeros_like(x)]

    finals = []
    for part in range(PARTS):
        pieces = [sums[part]] + [around(sums[part], k) for k in shifts]
        if part == 0:
            pieces, _ = lax.optimization_barrier((pieces, sums[1]))
        else:
            pieces, b_own = lax.optimization_barrier((pieces, b_own))
            b_other = core(b_own)
        g_own = jnp.concatenate(pieces, axis=0)
        g_own, finals = lax.optimization_barrier((g_own, finals))
        partial = weight_grad_of(x_turned, g_own, core(g_own), n)
        finals += over_reps(partial)
    sums, _ = lax.optimization_barrier((sums, partial))
    input_grad = input_grad_of(place, sums, w_own, w_other, b_own, b_other, n, rows)
    finals, input_grad = lax.optimization_barrier((finals, input_grad))
    grads = finish(place, *finals)
    return context[None], query_grad[None], input_grad[None], grads[0], grads[1]


def solution(mesh):
    return jax.shard_map(
        body,
        mesh=mesh,
        in_specs=(
            P(("groups", "rep", "fsdp"), "seq", None),
            P(("groups", "rep", "fsdp"), "seq", None),
            P(("seq", "fsdp"), None),
            P(("seq", "fsdp"), None),
            P(("groups", "rep", "fsdp"), "seq"),
            P(("groups", "rep", "fsdp"), "seq", None),
        ),
        out_specs=(
            P(("groups", "rep", "fsdp"), "seq", None),
            P(("groups", "rep", "fsdp"), "seq", None),
            P(("groups", "rep", "fsdp"), "seq", None),
            P(("groups", "seq", "fsdp"), None),
            P(("groups", "seq", "fsdp"), None),
        ),
        check_vma=False,
    )
```
